128 devices in a mesh: tm: 16 (over y, z_lo, core), tensor: 8 (over z_hi, x).
Axes of the slice: x: 4, y: 4, z: 4 (z_hi: 2, z_lo: 2; z = z_hi * 2 + z_lo), core: 2. Of those that a mesh axis runs over, the one named last changes fastest.
Arguments:
- activations: bfloat16 [16384, 3072], P(('tm', 'tensor')), may hold values from -6 to 6
- mod_gain: float32 [3072], replicated, may hold values from 0.1 to 1.9
- mod_shift: float32 [3072], replicated, may hold values from -3 to 3
- out_gate: float32 [3072], replicated, may hold values from 0.5 to 2
- qkv_weight: bfloat16 [3072, 24, 384], P(None, 'tensor'), may hold values from -0.109375 to 0.109375
- out_weight: bfloat16 [24, 128, 3072], P('tensor'), may hold values from -0.109375 to 0.109375
- tile_mask: int32 [64, 7, 4, 4], P('tm'), may hold values 0 or 1
- cotangent: bfloat16 [16384, 3072], P('tm'), may hold values from -6 to 6
Outputs:
- layer_out: bfloat16 [16384, 3072], P(('tm', 'tensor'))
- input_grad: bfloat16 [16384, 3072], P(('tm', 'tensor'))
The draws below stay inside these ranges and needn't reach their ends.
All inputs are finite; a program needn't handle non-finite values. No bound on the sum of `tile_mask` on one device may be relied on, other than what follows from the above.
Results may differ from the reference program's by a relative error of at most 0.015.
Values may be sent and summed in bfloat16 or wider, within the bound.
A program may use at most 320 MiB of HBM per device.

```python
import math
import jax
import jax.numpy as jnp
from jax import lax

D = 3072
HEADS = 24
HD = 128
FRAME = 256
TILE = 64
RADIUS = 3
FRAMES = 64
TOKENS = 16384
TILES = 4


def touch_ends(array, own_key, smallest, high):
    shape = array.shape
    place = [jax.random.randint(jax.random.fold_in(own_key, axis), (), 0, shape[axis]) for axis in range(len(shape))]
    array = array.at[tuple(place)].set(smallest)
    longest = shape.index(max(shape))
    place[longest] = (place[longest] + 1) % shape[longest]
    return array.at[tuple(place)].set(high)


def shard_levels(rng, extent, cuts, least, largest):
    def one(position, parts):
        steps = jax.random.uniform(jax.random.fold_in(jax.random.fold_in(rng, 6), position), (parts,), jnp.float32, least / len(cuts), largest / len(cuts))
        return jnp.repeat(jnp.exp(steps), extent[position] // parts).reshape((-1,) + (1,) * (len(extent) - position - 1))

    level = one(*cuts[0])
    for cut in cuts[1:]:
        level = level * one(*cut)
    return level


def normal_values(own_key, extent, scale, most, shards=(), held_as=jnp.bfloat16):
    gain = shard_levels(own_key, extent, shards, -0.22, 0.18) if shards else 1.0
    values = jax.random.normal(own_key, extent, jnp.float32) * scale * gain
    return jnp.minimum(jnp.maximum(values, -most), most).astype(held_as)


def setup_inputs(seed: int = 0) -> dict:
    key_list = jax.random.split(jax.random.key(seed), 9)
    return {
        "activations": normal_values(key_list[0], (TOKENS, D), 1.0, 6.0, ((0, 128),)),
        "mod_gain": jnp.clip(1.0 + 0.18 * jax.random.normal(key_list[1], (D,), jnp.float32), 0.1, 1.9),
        "mod_shift": normal_values(key_list[2], (D,), 0.5, 3.0, (), jnp.float32),
        "out_gate": jnp.clip(jnp.exp(jax.random.uniform(key_list[3], (D,), jnp.float32, math.log(0.5), math.log(2.0))), 0.5, 2.0),
        "qkv_weight": normal_values(key_list[4], (D, HEADS, 3 * HD), D ** -0.5, 0.109375, ((1, 8),)),
        "out_weight": normal_values(key_list[5], (HEADS, HD, D), D ** -0.5, 0.109375, ((0, 8),)),
        "tile_mask": touch_ends((jax.random.randint(key_list[6], (FRAMES, 2 * RADIUS + 1, TILES, TILES), 0, 2) < 1).astype(jnp.int32), jax.random.fold_in(key_list[6], 1), 0, 1),
        "cotangent": normal_values(key_list[7], (TOKENS, D), 1.0, 6.0, ((0, 16),)),
    }


EPSILON = 1e-06

def norm_rows(inputs, mod_gain, mod_shift):
    floated = inputs.astype(jnp.float32)
    row_mean = lax.optimization_barrier(jnp.mean(floated, axis=-1, keepdims=True))
    centered = floated - row_mean
    inverse = lax.rsqrt(lax.optimization_barrier(jnp.mean(centered * centered, axis=-1, keepdims=True)) + EPSILON)
    standard = centered * inverse
    return (standard, inverse, (standard * mod_gain + mod_shift).astype(jnp.bfloat16))

def norm_back(grad_norm, standard, inverse, mod_gain, cotangent):
    scaled_grad = grad_norm * mod_gain
    centered = scaled_grad - lax.optimization_barrier(jnp.mean(scaled_grad, axis=-1, keepdims=True))
    projected = standard * lax.optimization_barrier(jnp.mean(scaled_grad * standard, axis=-1, keepdims=True))
    return (cotangent.astype(jnp.float32) + inverse * (centered - projected)).astype(jnp.bfloat16)

def window_mask(tile_mask, first_frame, total_frames):
    expanded = jnp.repeat(jnp.repeat(tile_mask, TILE, axis=2), TILE, axis=3)
    frame_ids = lax.broadcasted_iota(jnp.int32, expanded.shape, 0) + first_frame
    offset_ids = lax.broadcasted_iota(jnp.int32, expanded.shape, 1)
    query_pos = lax.broadcasted_iota(jnp.int32, expanded.shape, 2)
    key_pos = lax.broadcasted_iota(jnp.int32, expanded.shape, 3)
    source = frame_ids + offset_ids - RADIUS
    diagonal = (offset_ids == RADIUS) & (query_pos // TILE == key_pos // TILE)
    inside = (source >= 0) & (source < total_frames)
    allowed = ((expanded == 1) | diagonal) & inside
    return jnp.transpose(allowed, (0, 2, 1, 3)).reshape(expanded.shape[0], expanded.shape[2], -1)

def window_rows(padded, frame_count, radius):
    stacked = jnp.stack([padded[offset:offset + frame_count] for offset in range(2 * radius + 1)], axis=1)
    return stacked.reshape(frame_count, -1, padded.shape[2], padded.shape[3])

def spread_windows(window_grads, frame_count, radius):
    by_offset = window_grads.reshape(frame_count, 2 * radius + 1, -1, window_grads.shape[2], window_grads.shape[3])
    summed = jnp.zeros((frame_count + 2 * radius,) + by_offset.shape[2:], jnp.float32)
    for offset in range(2 * radius + 1):
        summed = summed + jnp.pad(by_offset[:, offset], ((offset, 2 * radius - offset), (0, 0), (0, 0), (0, 0)))
    return summed

def attend(queries, window, allowed, score_scale):
    head_dim = queries.shape[-1]
    key_rows = window[..., :head_dim].astype(jnp.float32)
    value_rows = window[..., head_dim:].astype(jnp.float32)
    scores = jnp.einsum('fqhc,fkhc->fhqk', queries.astype(jnp.float32), key_rows) * score_scale
    exponent = jnp.where(allowed[:, None], jnp.exp(scores), 0.0)
    totals = lax.optimization_barrier(jnp.sum(exponent, axis=-1))
    numerator = jnp.einsum('fhqk,fkhc->fqhc', exponent.astype(jnp.bfloat16).astype(jnp.float32), value_rows)
    output = (numerator / jnp.transpose(totals, (0, 2, 1))[..., None]).astype(jnp.bfloat16)
    return (output, totals)

def attend_back(queries, window, allowed, totals, output, grad_out, score_scale):
    head_dim = queries.shape[-1]
    key_rows = window[..., :head_dim].astype(jnp.float32)
    value_rows = window[..., head_dim:].astype(jnp.float32)
    query_rows = queries.astype(jnp.float32)
    grad_rows = grad_out.astype(jnp.float32)
    scores = jnp.einsum('fqhc,fkhc->fhqk', query_rows, key_rows) * score_scale
    probability = jnp.where(allowed[:, None], jnp.exp(scores), 0.0) / totals[..., None]
    grad_values = jnp.einsum('fhqk,fqhc->fkhc', probability.astype(jnp.bfloat16).astype(jnp.float32), grad_rows)
    grad_probs = jnp.einsum('fqhc,fkhc->fhqk', grad_rows, value_rows)
    row_delta = jnp.einsum('fqhc,fqhc->fhq', grad_rows, output.astype(jnp.float32))
    grad_scores = (probability * (grad_probs - row_delta[..., None])).astype(jnp.bfloat16).astype(jnp.float32)
    grad_queries = (jnp.einsum('fhqk,fkhc->fqhc', grad_scores, key_rows) * score_scale).astype(jnp.bfloat16)
    grad_keys = jnp.einsum('fhqk,fqhc->fkhc', grad_scores, query_rows) * score_scale
    return (grad_queries, jnp.concatenate([grad_keys, grad_values], axis=-1))

def reference(activations, mod_gain, mod_shift, out_gate, qkv_weight, out_weight, tile_mask, cotangent):
    score_scale = HD ** (-0.5)
    standard, inverse, modulated = norm_rows(activations, mod_gain, mod_shift)
    joined_qkv = jnp.dot(modulated, qkv_weight.reshape(D, HEADS * 3 * HD), preferred_element_type=jnp.float32)
    joined_qkv = joined_qkv.astype(jnp.bfloat16).reshape(FRAMES, FRAME, HEADS, 3 * HD)
    queries = joined_qkv[..., :HD]
    padded = jnp.pad(joined_qkv[..., HD:], ((RADIUS, RADIUS), (0, 0), (0, 0), (0, 0)))
    allowed = window_mask(tile_mask, 0, FRAMES)
    head_queries = jnp.moveaxis(queries, 2, 0)[:, :, :, None]
    head_pairs = jnp.moveaxis(padded, 2, 0)[:, :, :, None]

    def forward_head(head_items):
        one_queries, one_pairs = head_items
        return attend(one_queries, window_rows(one_pairs, FRAMES, RADIUS), allowed, score_scale)
    head_outputs, head_totals = lax.map(forward_head, (head_queries, head_pairs))
    output = jnp.moveaxis(head_outputs[:, :, :, 0], 0, 2)
    flat_out = output.reshape(TOKENS, HEADS * HD)
    projection = jnp.dot(flat_out, out_weight.reshape(HEADS * HD, D), preferred_element_type=jnp.float32)
    layer_out = (activations.astype(jnp.float32) + out_gate * projection).astype(jnp.bfloat16)
    scaled = (cotangent.astype(jnp.float32) * out_gate).astype(jnp.bfloat16)
    grad_out = jnp.dot(scaled, out_weight.reshape(HEADS * HD, D).T, preferred_element_type=jnp.float32)
    grad_out = grad_out.astype(jnp.bfloat16).reshape(FRAMES, FRAME, HEADS, HD)
    head_grads = jnp.moveaxis(grad_out, 2, 0)[:, :, :, None]

    def backward_head(head_items):
        one_queries, one_pairs, one_totals, one_output, one_grad = head_items
        window = window_rows(one_pairs, FRAMES, RADIUS)
        grad_queries, window_grads = attend_back(one_queries, window, allowed, one_totals, one_output, one_grad, score_scale)
        return (grad_queries, spread_windows(window_grads, FRAMES, RADIUS))
    head_gq, head_spread = lax.map(backward_head, (head_queries, head_pairs, head_totals, head_outputs, head_grads))
    grad_queries = jnp.moveaxis(head_gq[:, :, :, 0], 0, 2)
    spread = jnp.moveaxis(head_spread[:, :, :, 0], 0, 2)
    grad_pairs = spread[RADIUS:RADIUS + FRAMES].astype(jnp.bfloat16)
    grad_joined = jnp.concatenate([grad_queries, grad_pairs], axis=-1).reshape(TOKENS, HEADS * 3 * HD)
    grad_norm = jnp.dot(grad_joined, qkv_weight.reshape(D, HEADS * 3 * HD).T, preferred_element_type=jnp.float32)
    input_grad = norm_back(grad_norm, standard, inverse, mod_gain, cotangent)
    return (layer_out, input_grad)
```

```python
import functools
import math

import jax
import jax.numpy as jnp
from jax import lax
from jax.experimental import pallas as pl
from jax.experimental.pallas import tpu as pltpu
from jax.sharding import PartitionSpec as P

FRAME = 256
TILE = 64
RADIUS = 3
SPAN = 2 * RADIUS + 1
HD = 128
EPSILON = 1e-06
MASKED = -1e30


def norm_rows(inputs, mod_gain, mod_shift):
    floated = inputs.astype(jnp.float32)
    row_mean = jnp.mean(floated, axis=-1, keepdims=True)
    centered = floated - row_mean
    inverse = lax.rsqrt(jnp.mean(centered * centered, axis=-1, keepdims=True) + EPSILON)
    standard = centered * inverse
    return (standard, inverse, (standard * mod_gain + mod_shift).astype(jnp.bfloat16))


def norm_back(grad_norm, standard, inverse, mod_gain, cotangent):
    scaled_grad = grad_norm * mod_gain
    centered = scaled_grad - jnp.mean(scaled_grad, axis=-1, keepdims=True)
    projected = standard * jnp.mean(scaled_grad * standard, axis=-1, keepdims=True)
    return (cotangent.astype(jnp.float32) + inverse * (centered - projected)).astype(jnp.bfloat16)


def mask_bias(tile_mask, first_frame, total_frames):
    frames = lax.broadcasted_iota(jnp.int32, tile_mask.shape, 0) + first_frame
    offsets = lax.broadcasted_iota(jnp.int32, tile_mask.shape, 1)
    query_tile = lax.broadcasted_iota(jnp.int32, tile_mask.shape, 2)
    key_tile = lax.broadcasted_iota(jnp.int32, tile_mask.shape, 3)
    source = frames + offsets - RADIUS
    diagonal = (offsets == RADIUS) & (query_tile == key_tile)
    allowed = ((tile_mask == 1) | diagonal) & (source >= 0) & (source < total_frames)
    bias = jnp.where(allowed, 0.0, MASKED).astype(jnp.float32)
    bias = jnp.transpose(bias, (0, 1, 3, 2))
    return jnp.repeat(bias, TILE, axis=3)


def dot(a, b, dims):
    return lax.dot_general(a, b, (dims, ((), ())), preferred_element_type=jnp.float32)


NN = ((1,), (0,))
NT = ((1,), (1,))


def attention_kernel(
    joined, low, high, grad_out, bias, out, grad_q, own, rims,
    keys, values, keys_t, values_t, exps, grad_k, grad_v,
):
    frame = pl.program_id(1)
    frames = pl.num_programs(1)
    block = 4 * FRAME
    rim = RADIUS * FRAME
    scale = HD ** (-0.5)

    @pl.when(frame == 0)
    def _():
        keys[0:rim, :] = low[0, :, 0:HD]
        keys[rim : rim + block, :] = joined[0, :, HD : 2 * HD]
        keys[rim + block :, :] = high[0, :, 0:HD]
        values[0:rim, :] = low[0, :, HD:]
        values[rim : rim + block, :] = joined[0, :, 2 * HD :]
        values[rim + block :, :] = high[0, :, HD:]
        for part in range(block // FRAME + 2 * RADIUS):
            rows = slice(part * FRAME, (part + 1) * FRAME)
            keys_t[part, :, :] = keys[rows, :].T
            values_t[part, :, :] = values[rows, :].T
        grad_k[...] = jnp.zeros_like(grad_k)
        grad_v[...] = jnp.zeros_like(grad_v)

    own_rows = pl.ds(pl.multiple_of(frame * FRAME, FRAME), FRAME)
    query = joined[0, own_rows, 0:HD]
    grads = grad_out[0, own_rows, :]

    totals = jnp.zeros((8, FRAME), jnp.float32)
    numer = jnp.zeros((HD, FRAME), jnp.float32)
    for offset in range(SPAN):
        rows = pl.ds(pl.multiple_of((frame + offset) * FRAME, FRAME), FRAME)
        scores = dot(keys[rows, :], query, NT) * (scale * math.log2(math.e))
        parts = []
        for tile in range(FRAME // TILE):
            line = bias[0, offset, tile : tile + 1, :]
            parts.append(jnp.exp2(scores[tile * TILE : (tile + 1) * TILE, :] + line))
        exponent = jnp.concatenate(parts, axis=0)
        exps[offset * FRAME : (offset + 1) * FRAME, :] = exponent
        totals += jnp.sum(exponent.reshape(FRAME // 8, 8, FRAME), axis=0)
        numer += dot(values_t[frame + offset], exponent.astype(jnp.bfloat16), NN)
    inverse = 1.0 / jnp.sum(totals, axis=0, keepdims=True)
    output = (numer * inverse).T.astype(jnp.bfloat16)
    out[0] = output
    product = grads.astype(jnp.float32) * output.astype(jnp.float32)
    delta = jnp.sum(product.T, axis=0, keepdims=True)

    grad_query = jnp.zeros((HD, FRAME), jnp.float32)
    for offset in range(SPAN):
        rows = pl.ds(pl.multiple_of((frame + offset) * FRAME, FRAME), FRAME)
        probability = exps[offset * FRAME : (offset + 1) * FRAME, :] * inverse
        grad_probs = dot(values[rows, :], grads, NT)
        grad_v[rows, :] += dot(probability.astype(jnp.bfloat16), grads, NN)
        grad_scores = (probability * (grad_probs - delta)).astype(jnp.bfloat16)
        grad_k[rows, :] += dot(grad_scores, query, NN)
        grad_query += dot(keys_t[frame + offset], grad_scores, NN)
    grad_q[0] = (grad_query * scale).T.astype(jnp.bfloat16)

    @pl.when(frame == frames - 1)
    def _():
        own[0, :, 0:HD] = grad_k[rim : rim + block, :] * scale
        own[0, :, HD:] = grad_v[rim : rim + block, :]
        rims[0, 0:rim, 0:HD] = (grad_k[0:rim, :] * scale).astype(jnp.bfloat16)
        rims[0, rim:, 0:HD] = (grad_k[rim + block :, :] * scale).astype(jnp.bfloat16)
        rims[0, 0:rim, HD:] = grad_v[0:rim, :].astype(jnp.bfloat16)
        rims[0, rim:, HD:] = grad_v[rim + block :, :].astype(jnp.bfloat16)


def attention(joined, low, high, grad_out, bias):
    heads, block, _ = joined.shape
    frames = block // FRAME
    rim = RADIUS * FRAME
    whole = block + 2 * rim
    per_head = lambda head, frame: (head, 0, 0)
    per_frame = lambda head, frame: (head, frame, 0)
    return pl.pallas_call(
        attention_kernel,
        grid=(heads, frames),
        out_shape=(
            jax.ShapeDtypeStruct((heads, block, HD), jnp.bfloat16),
            jax.ShapeDtypeStruct((heads, block, HD), jnp.bfloat16),
            jax.ShapeDtypeStruct((heads, block, 2 * HD), jnp.float32),
            jax.ShapeDtypeStruct((heads, 2 * rim, 2 * HD), jnp.bfloat16),
        ),
        in_specs=[
            pl.BlockSpec((1, block, 3 * HD), per_head),
            pl.BlockSpec((1, rim, 2 * HD), per_head),
            pl.BlockSpec((1, rim, 2 * HD), per_head),
            pl.BlockSpec((1, block, HD), per_head),
            pl.BlockSpec((1, SPAN, 4, FRAME), lambda head, frame: (frame, 0, 0, 0)),
        ],
        out_specs=(
            pl.BlockSpec((1, FRAME, HD), per_frame),
            pl.BlockSpec((1, FRAME, HD), per_frame),
            pl.BlockSpec((1, block, 2 * HD), per_head),
            pl.BlockSpec((1, 2 * rim, 2 * HD), per_head),
        ),
        scratch_shapes=[
            pltpu.VMEM((whole, HD), jnp.bfloat16),
            pltpu.VMEM((whole, HD), jnp.bfloat16),
            pltpu.VMEM((whole // FRAME, HD, FRAME), jnp.bfloat16),
            pltpu.VMEM((whole // FRAME, HD, FRAME), jnp.bfloat16),
            pltpu.VMEM((SPAN * FRAME, FRAME), jnp.float32),
            pltpu.VMEM((whole, HD), jnp.float32),
            pltpu.VMEM((whole, HD), jnp.float32),
        ],
        compiler_params=pltpu.CompilerParams(
            dimension_semantics=("arbitrary", "arbitrary"), vmem_limit_bytes=40 << 20
        ),
        name="attention",
    )(joined, low, high, grad_out, bias)


def on_device(
    activations, mod_gain, mod_shift, out_gate, qkv_weight, out_weight, tile_mask, cotangent
):
    shard_rows = activations.shape[0]
    group_rows = cotangent.shape[0]
    frame_count = tile_mask.shape[0]
    rim = RADIUS * FRAME
    standard, inverse, modulated = norm_rows(activations, mod_gain, mod_shift)
    rows_here = lax.all_gather(modulated, "tensor", tiled=True)
    weight = jnp.transpose(qkv_weight, (1, 0, 2))
    joined = jnp.einsum("rd,hdc->hrc", rows_here, weight, preferred_element_type=jnp.float32)
    joined = joined.astype(jnp.bfloat16)
    count = lax.axis_size("tm")
    upward = [(i, i + 1) for i in range(count - 1)]
    downward = [(i + 1, i) for i in range(count - 1)]
    low = lax.ppermute(joined[:, group_rows - rim :, HD:], "tm", upward)
    high = lax.ppermute(joined[:, :rim, HD:], "tm", downward)
    scaled = (cotangent.astype(jnp.float32) * out_gate).astype(jnp.bfloat16)
    grad_out = jnp.einsum("rd,hcd->hrc", scaled, out_weight, preferred_element_type=jnp.float32)
    grad_out = grad_out.astype(jnp.bfloat16)
    bias = mask_bias(tile_mask, lax.axis_index("tm") * frame_count, frame_count * count)
    output, grad_queries, own, rims = attention(joined, low, high, grad_out, bias)
    projection = lax.psum_scatter(
        jnp.einsum("hrc,hcd->rd", output, out_weight, preferred_element_type=jnp.float32).astype(
            jnp.bfloat16
        ),
        "tensor",
        scatter_dimension=0,
        tiled=True,
    ).astype(jnp.float32)
    layer_out = (activations.astype(jnp.float32) + out_gate * projection).astype(jnp.bfloat16)
    from_above = lax.ppermute(rims[:, :rim], "tm", downward).astype(jnp.float32)
    from_below = lax.ppermute(rims[:, rim:], "tm", upward).astype(jnp.float32)
    spare = group_rows - rim
    grad_pairs = (
        own
        + jnp.pad(from_below, ((0, 0), (0, spare), (0, 0)))
        + jnp.pad(from_above, ((0, 0), (spare, 0), (0, 0)))
    ).astype(jnp.bfloat16)
    grad_joined = jnp.concatenate([grad_queries, grad_pairs], axis=-1)
    grad_norm = lax.psum_scatter(
        jnp.einsum("hrc,hdc->rd", grad_joined, weight, preferred_element_type=jnp.float32).astype(
            jnp.bfloat16
        ),
        "tensor",
        scatter_dimension=0,
        tiled=True,
    ).astype(jnp.float32)
    own_cotangent = lax.dynamic_slice_in_dim(
        cotangent, lax.axis_index("tensor") * shard_rows, shard_rows, 0
    )
    input_grad = norm_back(grad_norm, standard, inverse, mod_gain, own_cotangent)
    return (layer_out, input_grad)


def solution(mesh):
    placed = (
        P(("tm", "tensor"), None),
        P(),
        P(),
        P(),
        P(None, "tensor", None),
        P("tensor", None, None),
        P("tm", None, None, None),
        P("tm", None),
    )
    return jax.shard_map(
        on_device,
        mesh=mesh,
        in_specs=placed,
        out_specs=(P(("tm", "tensor"), None), P(("tm", "tensor"), None)),
        check_vma=False,
    )
```

```python
import functools
import math

import jax
import jax.numpy as jnp
from jax import lax
from jax.experimental import pallas as pl
from jax.experimental.pallas import tpu as pltpu
from jax.sharding import PartitionSpec as P

FRAME = 256
TILE = 64
RADIUS = 3
SPAN = 2 * RADIUS + 1
HD = 128
EPSILON = 1e-06
MASKED = -1e30


def norm_rows(inputs, mod_gain, mod_shift):
    floated = inputs.astype(jnp.float32)
    row_mean = jnp.mean(floated, axis=-1, keepdims=True)
    centered = floated - row_mean
    inverse = lax.rsqrt(jnp.mean(centered * centered, axis=-1, keepdims=True) + EPSILON)
    standard = centered * inverse
    return (standard, inverse, (standard * mod_gain + mod_shift).astype(jnp.bfloat16))


def norm_back(grad_norm, standard, inverse, mod_gain, cotangent):
    scaled_grad = grad_norm * mod_gain
    centered = scaled_grad - jnp.mean(scaled_grad, axis=-1, keepdims=True)
    projected = standard * jnp.mean(scaled_grad * standard, axis=-1, keepdims=True)
    return (cotangent.astype(jnp.float32) + inverse * (centered - projected)).astype(jnp.bfloat16)


def mask_bias(tile_mask, first_frame, total_frames):
    frames = lax.broadcasted_iota(jnp.int32, tile_mask.shape, 0) + first_frame
    offsets = lax.broadcasted_iota(jnp.int32, tile_mask.shape, 1)
    query_tile = lax.broadcasted_iota(jnp.int32, tile_mask.shape, 2)
    key_tile = lax.broadcasted_iota(jnp.int32, tile_mask.shape, 3)
    source = frames + offsets - RADIUS
    diagonal = (offsets == RADIUS) & (query_tile == key_tile)
    allowed = ((tile_mask == 1) | diagonal) & (source >= 0) & (source < total_frames)
    bias = jnp.where(allowed, 0.0, MASKED).astype(jnp.float32)
    bias = jnp.transpose(bias, (0, 1, 3, 2))
    return jnp.repeat(bias, TILE, axis=3)


def dot(a, b, dims):
    return lax.dot_general(a, b, (dims, ((), ())), preferred_element_type=jnp.float32)


NN = ((1,), (0,))
NT = ((1,), (1,))


def attention_kernel(
    joined, low, high, grad_out, bias, out, grad_q, own, rims,
    keys, values, keys_t, values_t, exps, grad_k, grad_v,
):
    frame = pl.program_id(1)
    frames = pl.num_programs(1)
    block = 4 * FRAME
    rim = RADIUS * FRAME
    scale = HD ** (-0.5)

    @pl.when(frame == 0)
    def _():
        keys[0:rim, :] = low[0, :, 0:HD]
        keys[rim : rim + block, :] = joined[0, :, HD : 2 * HD]
        keys[rim + block :, :] = high[0, :, 0:HD]
        values[0:rim, :] = low[0, :, HD:]
        values[rim : rim + block, :] = joined[0, :, 2 * HD :]
        values[rim + block :, :] = high[0, :, HD:]
        for part in range(block // FRAME + 2 * RADIUS):
            rows = slice(part * FRAME, (part + 1) * FRAME)
            keys_t[part, :, :] = keys[rows, :].T
            values_t[part, :, :] = values[rows, :].T
        grad_k[...] = jnp.zeros_like(grad_k)
        grad_v[...] = jnp.zeros_like(grad_v)

    own_rows = pl.ds(pl.multiple_of(frame * FRAME, FRAME), FRAME)
    query = joined[0, own_rows, 0:HD]
    grads = grad_out[0, own_rows, :]

    totals = jnp.zeros((8, FRAME), jnp.float32)
    numer = jnp.zeros((HD, FRAME), jnp.float32)
    for offset in range(SPAN):
        rows = pl.ds(pl.multiple_of((frame + offset) * FRAME, FRAME), FRAME)
        scores = dot(keys[rows, :], query, NT) * (scale * math.log2(math.e))
        parts = []
        for tile in range(FRAME // TILE):
            line = bias[0, offset, tile : tile + 1, :]
            parts.append(jnp.exp2(scores[tile * TILE : (tile + 1) * TILE, :] + line))
        exponent = jnp.concatenate(parts, axis=0)
        exps[offset * FRAME : (offset + 1) * FRAME, :] = exponent
        totals += jnp.sum(exponent.reshape(FRAME // 8, 8, FRAME), axis=0)
        numer += dot(values_t[frame + offset], exponent.astype(jnp.bfloat16), NN)
    inverse = 1.0 / jnp.sum(totals, axis=0, keepdims=True)
    output = (numer * inverse).T.astype(jnp.bfloat16)
    out[0] = output
    product = grads.astype(jnp.float32) * output.astype(jnp.float32)
    delta = jnp.sum(product.T, axis=0, keepdims=True)

    grad_query = jnp.zeros((HD, FRAME), jnp.float32)
    for offset in range(SPAN):
        rows = pl.ds(pl.multiple_of((frame + offset) * FRAME, FRAME), FRAME)
        probability = exps[offset * FRAME : (offset + 1) * FRAME, :] * inverse
        grad_probs = dot(values[rows, :], grads, NT)
        grad_v[rows, :] += dot(probability.astype(jnp.bfloat16), grads, NN)
        grad_scores = (probability * (grad_probs - delta)).astype(jnp.bfloat16)
        grad_k[rows, :] += dot(grad_scores, query, NN)
        grad_query += dot(keys_t[frame + offset], grad_scores, NN)
    grad_q[0] = (grad_query * scale).T.astype(jnp.bfloat16)

    @pl.when(frame == frames - 1)
    def _():
        own[0, :, 0:HD] = grad_k[rim : rim + block, :] * scale
        own[0, :, HD:] = grad_v[rim : rim + block, :]
        rims[0, 0:rim, 0:HD] = (grad_k[0:rim, :] * scale).astype(jnp.bfloat16)
        rims[0, rim:, 0:HD] = (grad_k[rim + block :, :] * scale).astype(jnp.bfloat16)
        rims[0, 0:rim, HD:] = grad_v[0:rim, :].astype(jnp.bfloat16)
        rims[0, rim:, HD:] = grad_v[rim + block :, :].astype(jnp.bfloat16)


def attention(joined, low, high, grad_out, bias):
    heads, block, _ = joined.shape
    frames = block // FRAME
    rim = RADIUS * FRAME
    whole = block + 2 * rim
    per_head = lambda head, frame: (head, 0, 0)
    per_frame = lambda head, frame: (head, frame, 0)
    return pl.pallas_call(
        attention_kernel,
        grid=(heads, frames),
        out_shape=(
            jax.ShapeDtypeStruct((heads, block, HD), jnp.bfloat16),
            jax.ShapeDtypeStruct((heads, block, HD), jnp.bfloat16),
            jax.ShapeDtypeStruct((heads, block, 2 * HD), jnp.float32),
            jax.ShapeDtypeStruct((heads, 2 * rim, 2 * HD), jnp.bfloat16),
        ),
        in_specs=[
            pl.BlockSpec((1, block, 3 * HD), per_head),
            pl.BlockSpec((1, rim, 2 * HD), per_head),
            pl.BlockSpec((1, rim, 2 * HD), per_head),
            pl.BlockSpec((1, block, HD), per_head),
            pl.BlockSpec((1, SPAN, 4, FRAME), lambda head, frame: (frame, 0, 0, 0)),
        ],
        out_specs=(
            pl.BlockSpec((1, FRAME, HD), per_frame),
            pl.BlockSpec((1, FRAME, HD), per_frame),
            pl.BlockSpec((1, block, 2 * HD), per_head),
            pl.BlockSpec((1, 2 * rim, 2 * HD), per_head),
        ),
        scratch_shapes=[
            pltpu.VMEM((whole, HD), jnp.bfloat16),
            pltpu.VMEM((whole, HD), jnp.bfloat16),
            pltpu.VMEM((whole // FRAME, HD, FRAME), jnp.bfloat16),
            pltpu.VMEM((whole // FRAME, HD, FRAME), jnp.bfloat16),
            pltpu.VMEM((SPAN * FRAME, FRAME), jnp.float32),
            pltpu.VMEM((whole, HD), jnp.float32),
            pltpu.VMEM((whole, HD), jnp.float32),
        ],
        compiler_params=pltpu.CompilerParams(
            dimension_semantics=("arbitrary", "arbitrary"), vmem_limit_bytes=40 << 20
        ),
        name="attention",
    )(joined, low, high, grad_out, bias)


SIXTH = 512
LOW = (0, 3)
HIGH = (3, 6)


def cols(span):
    return slice(span[0] * SIXTH, span[1] * SIXTH)


def ring_places():
    me = lax.axis_index("tensor")
    z, x = me // 4, me % 4

    def place(other, shift):
        return ((z + other) % 2) * 4 + (x + shift) % 4

    return place


def meet(neighbours):
    barrier = pltpu.get_barrier_semaphore()
    for neighbour in neighbours:
        pl.semaphore_signal(
            barrier, inc=1, device_id={"tensor": neighbour}, device_id_type=pl.DeviceIdType.MESH
        )
    pl.semaphore_wait(barrier, len(neighbours))


def gather_kernel(block, out, send, recv, own_sem):
    place = ring_places()
    up, down, across = place(0, 1), place(0, -1), place(1, 0)
    size = block.shape[0]

    def rows(other, shift):
        return pl.ds(pl.multiple_of(place(other, shift) * size, size), size)

    meet((up, down, across))
    started = []

    def push(number, target, source, other, shift, span):
        where = out.at[rows(other, shift), cols(span)]
        if source is None:
            source = where
        else:
            source = source.at[:, cols(span)]
        copy = pltpu.make_async_remote_copy(
            src_ref=source,
            dst_ref=where,
            send_sem=send.at[number],
            recv_sem=recv.at[number],
            device_id={"tensor": target},
            device_id_type=pl.DeviceIdType.MESH,
        )
        copy.start()
        started.append(copy)

    def arrived(number, other, shift, span):
        where = out.at[rows(other, shift), cols(span)]
        pltpu.make_async_remote_copy(
            src_ref=where,
            dst_ref=where,
            send_sem=send.at[number],
            recv_sem=recv.at[number],
            device_id={"tensor": up},
            device_id_type=pl.DeviceIdType.MESH,
        ).wait_recv()

    push(0, up, block, 0, 0, LOW)
    push(5, down, block, 0, 0, HIGH)
    push(10, across, block, 0, 0, HIGH)
    push(1, up, block, 0, 0, HIGH)
    push(6, down, block, 0, 0, LOW)
    push(11, across, block, 0, 0, LOW)
    own = pltpu.make_async_copy(block, out.at[rows(0, 0), :], own_sem)
    own.start()
    arrived(0, 0, -1, LOW)
    push(2, up, None, 0, -1, LOW)
    push(12, across, None, 0, -1, LOW)
    arrived(5, 0, 1, HIGH)
    push(7, down, None, 0, 1, HIGH)
    arrived(10, 1, 0, HIGH)
    push(3, up, None, 1, 0, HIGH)
    push(8, down, None, 1, 0, HIGH)
    arrived(6, 0, 1, LOW)
    push(13, across, None, 0, 1, LOW)
    arrived(12, 1, -1, LOW)
    push(4, up, None, 1, -1, (0, 2))
    arrived(7, 0, 2, HIGH)
    push(14, across, None, 0, 2, (4, 6))
    arrived(13, 1, 1, LOW)
    arrived(8, 1, 1, HIGH)
    push(9, down, None, 1, 1, (2, 4))
    arrived(1, 0, -1, HIGH)
    arrived(11, 1, 0, LOW)
    arrived(2, 0, 2, LOW)
    arrived(3, 1, -1, HIGH)
    arrived(4, 1, 2, (0, 2))
    arrived(9, 1, 2, (2, 4))
    arrived(14, 1, 2, (4, 6))
    for copy in started:
        copy.wait_send()
    own.wait()


def gather_rows(block):
    size, width = block.shape
    return pl.pallas_call(
        gather_kernel,
        out_shape=jax.ShapeDtypeStruct((8 * size, width), block.dtype),
        in_specs=[pl.BlockSpec(memory_space=pltpu.VMEM)],
        out_specs=pl.BlockSpec(memory_space=pltpu.VMEM),
        scratch_shapes=[
            pltpu.SemaphoreType.DMA((15,)),
            pltpu.SemaphoreType.DMA((15,)),
            pltpu.SemaphoreType.DMA(()),
        ],
        compiler_params=pltpu.CompilerParams(
            collective_id=0, has_side_effects=True, vmem_limit_bytes=40 << 20
        ),
        cost_estimate=pl.CostEstimate(
            flops=0, bytes_accessed=180 << 20, transcendentals=0
        ),
        name="gather_rows",
    )(block)


def scatter_kernel(partial, out, landing, staged, send, recv):
    place = ring_places()
    up, down, across = place(0, 1), place(0, -1), place(1, 0)
    size = out.shape[0]

    def rows(other, shift):
        return pl.ds(pl.multiple_of(place(other, shift) * size, size), size)

    meet((up, down, across))
    started = []

    def push(number, target, source, width):
        copy = pltpu.make_async_remote_copy(
            src_ref=source,
            dst_ref=landing.at[number, :, 0 : width * SIXTH],
            send_sem=send.at[number],
            recv_sem=recv.at[number],
            device_id={"tensor": target},
            device_id_type=pl.DeviceIdType.MESH,
        )
        copy.start()
        started.append(copy)

    def plain(number, target, other, shift, span):
        push(number, target, partial.at[rows(other, shift), cols(span)], span[1] - span[0])

    def arrived(number, width=3):
        where = landing.at[number, :, 0 : width * SIXTH]
        pltpu.make_async_remote_copy(
            src_ref=where,
            dst_ref=where,
            send_sem=send.at[number],
            recv_sem=recv.at[number],
            device_id={"tensor": up},
            device_id_type=pl.DeviceIdType.MESH,
        ).wait_recv()

    def summed(number, target, slot, other, shift, span, parts):
        for piece in range(span[0], span[1]):
            total = partial[rows(other, shift), cols((piece, piece + 1))].astype(jnp.float32)
            for landed, first, over in parts:
                if over[0] <= piece < over[1]:
                    total += landing[landed, :, cols((piece - first, piece - first + 1))].astype(jnp.float32)
            staged[slot, :, cols((piece - span[0], piece - span[0] + 1))] = total.astype(jnp.bfloat16)
        push(number, target, staged.at[slot], 3)

    plain(0, down, 1, 2, (0, 2))
    plain(5, up, 1, 2, (2, 4))
    plain(10, across, 1, 2, (4, 6))
    plain(1, down, 1, -1, HIGH)
    plain(2, down, 0, 2, LOW)
    plain(3, down, 0, -1, HIGH)
    arrived(5, 2)
    summed(6, up, 0, 1, 1, HIGH, ((5, 2, (2, 4)),))
    arrived(0, 2)
    summed(11, across, 1, 1, -1, LOW, ((0, 0, (0, 2)),))
    arrived(10, 2)
    summed(7, up, 2, 0, 2, HIGH, ((10, 4, (4, 6)),))
    summed(12, across, 3, 1, 1, LOW, ((5, 2, (2, 4)),))
    plain(13, across, 1, 0, LOW)
    arrived(2)
    arrived(11)
    summed(4, down, 4, 0, -1, LOW, ((2, 0, LOW), (11, 0, LOW)))
    arrived(12)
    summed(8, up, 5, 0, 1, LOW, ((12, 0, LOW),))
    arrived(7)
    summed(9, up, 6, 0, 1, HIGH, ((7, 3, HIGH),))
    arrived(1)
    arrived(6)
    summed(14, across, 7, 1, 0, HIGH, ((1, 3, HIGH), (6, 3, HIGH)))
    arrived(4)
    arrived(8)
    arrived(13)
    for piece in range(3):
        total = partial[rows(0, 0), cols((piece, piece + 1))].astype(jnp.float32)
        for landed in (4, 8, 13):
            total += landing[landed, :, cols((piece, piece + 1))].astype(jnp.float32)
        out[:, cols((piece, piece + 1))] = total
    arrived(3)
    arrived(9)
    arrived(14)
    for piece in range(3):
        total = partial[rows(0, 0), cols((piece + 3, piece + 4))].astype(jnp.float32)
        for landed in (3, 9, 14):
            total += landing[landed, :, cols((piece, piece + 1))].astype(jnp.float32)
        out[:, cols((piece + 3, piece + 4))] = total
    for copy in started:
        copy.wait_send()


def scatter_rows(partial, collective_id, name):
    height, width = partial.shape
    size = height // 8
    return pl.pallas_call(
        scatter_kernel,
        out_shape=jax.ShapeDtypeStruct((size, width), jnp.float32),
        in_specs=[pl.BlockSpec(memory_space=pltpu.VMEM)],
        out_specs=pl.BlockSpec(memory_space=pltpu.VMEM),
        scratch_shapes=[
            pltpu.VMEM((15, size, width // 2), jnp.bfloat16),
            pltpu.VMEM((8, size, width // 2), jnp.bfloat16),
            pltpu.SemaphoreType.DMA((15,)),
            pltpu.SemaphoreType.DMA((15,)),
        ],
        compiler_params=pltpu.CompilerParams(
            collective_id=collective_id, has_side_effects=True, vmem_limit_bytes=40 << 20
        ),
        cost_estimate=pl.CostEstimate(
            flops=0, bytes_accessed=180 << 20, transcendentals=0
        ),
        name=name,
    )(partial)


def on_device(
    activations, mod_gain, mod_shift, out_gate, qkv_weight, out_weight, tile_mask, cotangent
):
    shard_rows = activations.shape[0]
    group_rows = cotangent.shape[0]
    frame_count = tile_mask.shape[0]
    rim = RADIUS * FRAME
    standard, inverse, modulated = norm_rows(activations, mod_gain, mod_shift)
    rows_here = gather_rows(modulated)
    weight = jnp.transpose(qkv_weight, (1, 0, 2))
    joined = jnp.einsum("rd,hdc->hrc", rows_here, weight, preferred_element_type=jnp.float32)
    joined = joined.astype(jnp.bfloat16)
    count = lax.axis_size("tm")
    upward = [(i, i + 1) for i in range(count - 1)]
    downward = [(i + 1, i) for i in range(count - 1)]
    low = lax.ppermute(joined[:, group_rows - rim :, HD:], "tm", upward)
    high = lax.ppermute(joined[:, :rim, HD:], "tm", downward)
    scaled = (cotangent.astype(jnp.float32) * out_gate).astype(jnp.bfloat16)
    grad_out = jnp.einsum("rd,hcd->hrc", scaled, out_weight, preferred_element_type=jnp.float32)
    grad_out = grad_out.astype(jnp.bfloat16)
    bias = mask_bias(tile_mask, lax.axis_index("tm") * frame_count, frame_count * count)
    output, grad_queries, own, rims = attention(joined, low, high, grad_out, bias)
    projected = jnp.einsum("hrc,hcd->rd", output, out_weight, preferred_element_type=jnp.float32)
    projection = scatter_rows(projected.astype(jnp.bfloat16), 1, "scatter_out")
    layer_out = (activations.astype(jnp.float32) + out_gate * projection).astype(jnp.bfloat16)
    from_above = lax.ppermute(rims[:, :rim], "tm", downward).astype(jnp.float32)
    from_below = lax.ppermute(rims[:, rim:], "tm", upward).astype(jnp.float32)
    spare = group_rows - rim
    grad_pairs = (
        own
        + jnp.pad(from_below, ((0, 0), (0, spare), (0, 0)))
        + jnp.pad(from_above, ((0, 0), (spare, 0), (0, 0)))
    ).astype(jnp.bfloat16)
    grad_joined = jnp.concatenate([grad_queries, grad_pairs], axis=-1)
    grad_rows = jnp.einsum("hrc,hdc->rd", grad_joined, weight, preferred_element_type=jnp.float32)
    grad_norm = scatter_rows(grad_rows.astype(jnp.bfloat16), 2, "scatter_grad")
    own_cotangent = lax.dynamic_slice_in_dim(
        cotangent, lax.axis_index("tensor") * shard_rows, shard_rows, 0
    )
    input_grad = norm_back(grad_norm, standard, inverse, mod_gain, own_cotangent)
    return (layer_out, input_grad)


def solution(mesh):
    placed = (
        P(("tm", "tensor"), None),
        P(),
        P(),
        P(),
        P(None, "tensor", None),
        P("tensor", None, None),
        P("tm", None, None, None),
        P("tm", None),
    )
    return jax.shard_map(
        on_device,
        mesh=mesh,
        in_specs=placed,
        out_specs=(P(("tm", "tensor"), None), P(("tm", "tensor"), None)),
        check_vma=False,
    )
```

```python
import functools
import math

import jax
import jax.numpy as jnp
from jax import lax
from jax.experimental import pallas as pl
from jax.experimental.pallas import tpu as pltpu
from jax.sharding import PartitionSpec as P

FRAME = 256
TILE = 64
RADIUS = 3
SPAN = 2 * RADIUS + 1
HD = 128
EPSILON = 1e-06
MASKED = -1e30
HELD = 3


def norm_rows(inputs, mod_gain, mod_shift):
    floated = inputs.astype(jnp.float32)
    row_mean = jnp.mean(floated, axis=-1, keepdims=True)
    centered = floated - row_mean
    inverse = lax.rsqrt(jnp.mean(centered * centered, axis=-1, keepdims=True) + EPSILON)
    standard = centered * inverse
    return (standard, inverse, (standard * mod_gain + mod_shift).astype(jnp.bfloat16))


def norm_back(grad_norm, standard, inverse, mod_gain, cotangent):
    scaled_grad = grad_norm * mod_gain
    centered = scaled_grad - jnp.mean(scaled_grad, axis=-1, keepdims=True)
    projected = standard * jnp.mean(scaled_grad * standard, axis=-1, keepdims=True)
    return (cotangent.astype(jnp.float32) + inverse * (centered - projected)).astype(jnp.bfloat16)


def mask_bias(tile_mask, first_frame, total_frames):
    frames = lax.broadcasted_iota(jnp.int32, tile_mask.shape, 0) + first_frame
    offsets = lax.broadcasted_iota(jnp.int32, tile_mask.shape, 1)
    query_tile = lax.broadcasted_iota(jnp.int32, tile_mask.shape, 2)
    key_tile = lax.broadcasted_iota(jnp.int32, tile_mask.shape, 3)
    source = frames + offsets - RADIUS
    diagonal = (offsets == RADIUS) & (query_tile == key_tile)
    allowed = ((tile_mask == 1) | diagonal) & (source >= 0) & (source < total_frames)
    bias = jnp.where(allowed, 0.0, MASKED).astype(jnp.float32)
    return jnp.transpose(bias, (0, 1, 3, 2)).reshape(-1)


def dot(a, b, dims):
    return lax.dot_general(a, b, (dims, ((), ())), preferred_element_type=jnp.float32)


NN = ((1,), (0,))
NT = ((1,), (1,))


def attention_kernel(
    bias, joined, grad_out, out, grad_q, grad_pairs,
    keys, values, keys_t, values_t, exps, grad_k, grad_v, own, halo, rims, landed,
    halo_send, halo_recv, rims_send, rims_recv,
):
    head = pl.program_id(0)
    frame = pl.program_id(1)
    heads = pl.num_programs(0)
    frames = pl.num_programs(1)
    block = 4 * FRAME
    rim = RADIUS * FRAME
    spare = block - rim
    scale = HD ** (-0.5)
    me = lax.axis_index("tm")
    count = lax.axis_size("tm")
    above, below = lax.rem(me + 1, count), lax.rem(me + count - 1, count)

    def halo_copy(which, side):
        rows = slice(spare, block) if side == 0 else slice(0, rim)
        return pltpu.make_async_remote_copy(
            src_ref=joined.at[which, rows, HD : 3 * HD],
            dst_ref=halo.at[which, side],
            send_sem=halo_send.at[which, side],
            recv_sem=halo_recv.at[which, side],
            device_id={"tm": above if side == 0 else below},
            device_id_type=pl.DeviceIdType.MESH,
        )

    def rims_copy(which, side):
        return pltpu.make_async_remote_copy(
            src_ref=rims.at[which, side],
            dst_ref=landed.at[which, side],
            send_sem=rims_send.at[which, side],
            recv_sem=rims_recv.at[which, side],
            device_id={"tm": above if side == 0 else below},
            device_id_type=pl.DeviceIdType.MESH,
        )

    @pl.when((head == 0) & (frame == 0))
    def _():
        barrier = pltpu.get_barrier_semaphore()
        for neighbour in (above, below):
            pl.semaphore_signal(
                barrier, inc=1, device_id={"tm": neighbour}, device_id_type=pl.DeviceIdType.MESH
            )
        pl.semaphore_wait(barrier, 2)
        for which in range(HELD):
            for side in range(2):
                halo_copy(which, side).start()

    @pl.when(frame == 0)
    def _():
        keys[rim : rim + block, :] = joined[head, :, HD : 2 * HD]
        values[rim : rim + block, :] = joined[head, :, 2 * HD :]
        grad_k[...] = jnp.zeros_like(grad_k)
        grad_v[...] = jnp.zeros_like(grad_v)
        for which in range(HELD):

            @pl.when(head == which)
            def _():
                for side in range(2):
                    halo_copy(which, side).wait_recv()
                keys[0:rim, :] = halo[which, 0, :, 0:HD]
                keys[rim + block :, :] = halo[which, 1, :, 0:HD]
                values[0:rim, :] = halo[which, 0, :, HD:]
                values[rim + block :, :] = halo[which, 1, :, HD:]

        for part in range(block // FRAME + 2 * RADIUS):
            rows = slice(part * FRAME, (part + 1) * FRAME)
            keys_t[part, :, :] = keys[rows, :].T
            values_t[part, :, :] = values[rows, :].T

    query_tile = lax.broadcasted_iota(jnp.int32, (1, FRAME), 1) // TILE

    def bias_line(offset, tile):
        first = (frame * SPAN + offset) * 16 + tile * 4
        line = jnp.full((1, FRAME), bias[first], jnp.float32)
        for other in range(1, 4):
            line = jnp.where(query_tile == other, bias[first + other], line)
        return line

    own_rows = pl.ds(pl.multiple_of(frame * FRAME, FRAME), FRAME)
    query = joined[head, own_rows, 0:HD]
    grads = grad_out[0, own_rows, :]

    totals = jnp.zeros((8, FRAME), jnp.float32)
    numer = jnp.zeros((HD, FRAME), jnp.float32)
    for offset in range(SPAN):
        rows = pl.ds(pl.multiple_of((frame + offset) * FRAME, FRAME), FRAME)
        scores = dot(keys[rows, :], query, NT) * (scale * math.log2(math.e))
        parts = []
        for tile in range(FRAME // TILE):
            line = bias_line(offset, tile)
            parts.append(jnp.exp2(scores[tile * TILE : (tile + 1) * TILE, :] + line))
        exponent = jnp.concatenate(parts, axis=0)
        exps[offset * FRAME : (offset + 1) * FRAME, :] = exponent
        totals += jnp.sum(exponent.reshape(FRAME // 8, 8, FRAME), axis=0)
        numer += dot(values_t[frame + offset], exponent.astype(jnp.bfloat16), NN)
    inverse = 1.0 / jnp.sum(totals, axis=0, keepdims=True)
    output = (numer * inverse).T.astype(jnp.bfloat16)
    out[0] = output
    product = grads.astype(jnp.float32) * output.astype(jnp.float32)
    delta = jnp.sum(product.T, axis=0, keepdims=True)

    grad_query = jnp.zeros((HD, FRAME), jnp.float32)
    for offset in range(SPAN):
        rows = pl.ds(pl.multiple_of((frame + offset) * FRAME, FRAME), FRAME)
        probability = exps[offset * FRAME : (offset + 1) * FRAME, :] * inverse
        grad_probs = dot(values[rows, :], grads, NT)
        grad_v[rows, :] += dot(probability.astype(jnp.bfloat16), grads, NN)
        grad_scores = (probability * (grad_probs - delta)).astype(jnp.bfloat16)
        grad_k[rows, :] += dot(grad_scores, query, NN)
        grad_query += dot(keys_t[frame + offset], grad_scores, NN)
    grad_q[0] = (grad_query * scale).T.astype(jnp.bfloat16)

    @pl.when(frame == frames - 1)
    def _():
        for which in range(HELD):

            @pl.when(head == which)
            def _():
                own[which, :, 0:HD] = grad_k[rim : rim + block, :] * scale
                own[which, :, HD:] = grad_v[rim : rim + block, :]
                rims[which, 1, :, 0:HD] = (grad_k[0:rim, :] * scale).astype(jnp.bfloat16)
                rims[which, 0, :, 0:HD] = (grad_k[rim + block :, :] * scale).astype(jnp.bfloat16)
                rims[which, 1, :, HD:] = grad_v[0:rim, :].astype(jnp.bfloat16)
                rims[which, 0, :, HD:] = grad_v[rim + block :, :].astype(jnp.bfloat16)
                for side in range(2):
                    rims_copy(which, side).start()

    @pl.when((head == heads - 1) & (frame == frames - 1))
    def _():
        for which in range(HELD):
            for side in range(2):
                rims_copy(which, side).wait_recv()
            own[which, 0:rim, :] += landed[which, 0].astype(jnp.float32)
            own[which, spare:, :] += landed[which, 1].astype(jnp.float32)
            grad_pairs[which, :, :] = own[which, :, :].astype(jnp.bfloat16)
        for which in range(HELD):
            for side in range(2):
                halo_copy(which, side).wait_send()
                rims_copy(which, side).wait_send()


def attention(joined, grad_out, bias):
    heads, block, _ = joined.shape
    frames = block // FRAME
    rim = RADIUS * FRAME
    whole = block + 2 * rim
    per_head = lambda head, frame: (head, 0, 0)
    per_frame = lambda head, frame: (head, frame, 0)
    constant = lambda head, frame: (0, 0, 0)
    return pl.pallas_call(
        attention_kernel,
        grid=(heads, frames),
        out_shape=(
            jax.ShapeDtypeStruct((heads, block, HD), jnp.bfloat16),
            jax.ShapeDtypeStruct((heads, block, HD), jnp.bfloat16),
            jax.ShapeDtypeStruct((heads, block, 2 * HD), jnp.bfloat16),
        ),
        in_specs=[
            pl.BlockSpec(memory_space=pltpu.SMEM),
            pl.BlockSpec((heads, block, 3 * HD), constant),
            pl.BlockSpec((1, block, HD), per_head),
        ],
        out_specs=(
            pl.BlockSpec((1, FRAME, HD), per_frame),
            pl.BlockSpec((1, FRAME, HD), per_frame),
            pl.BlockSpec((heads, block, 2 * HD), constant),
        ),
        scratch_shapes=[
            pltpu.VMEM((whole, HD), jnp.bfloat16),
            pltpu.VMEM((whole, HD), jnp.bfloat16),
            pltpu.VMEM((whole // FRAME, HD, FRAME), jnp.bfloat16),
            pltpu.VMEM((whole // FRAME, HD, FRAME), jnp.bfloat16),
            pltpu.VMEM((SPAN * FRAME, FRAME), jnp.float32),
            pltpu.VMEM((whole, HD), jnp.float32),
            pltpu.VMEM((whole, HD), jnp.float32),
            pltpu.VMEM((heads, block, 2 * HD), jnp.float32),
            pltpu.VMEM((heads, 2, rim, 2 * HD), jnp.bfloat16),
            pltpu.VMEM((heads, 2, rim, 2 * HD), jnp.bfloat16),
            pltpu.VMEM((heads, 2, rim, 2 * HD), jnp.bfloat16),
            pltpu.SemaphoreType.DMA((heads, 2)),
            pltpu.SemaphoreType.DMA((heads, 2)),
            pltpu.SemaphoreType.DMA((heads, 2)),
            pltpu.SemaphoreType.DMA((heads, 2)),
        ],
        compiler_params=pltpu.CompilerParams(
            dimension_semantics=("arbitrary", "arbitrary"),
            collective_id=3,
            has_side_effects=True,
            vmem_limit_bytes=40 << 20,
        ),
        name="attention",
    )(bias, joined, grad_out)


SIXTH = 512
LOW = (0, 3)
HIGH = (3, 6)


def cols(span):
    return slice(span[0] * SIXTH, span[1] * SIXTH)


def ring_places():
    me = lax.axis_index("tensor")
    z, x = me // 4, me % 4

    def place(other, shift):
        return ((z + other) % 2) * 4 + (x + shift) % 4

    return place


def meet(neighbours):
    barrier = pltpu.get_barrier_semaphore()
    for neighbour in neighbours:
        pl.semaphore_signal(
            barrier, inc=1, device_id={"tensor": neighbour}, device_id_type=pl.DeviceIdType.MESH
        )
    pl.semaphore_wait(barrier, len(neighbours))


def gather_kernel(block, out, send, recv, own_sem):
    place = ring_places()
    up, down, across = place(0, 1), place(0, -1), place(1, 0)
    size = block.shape[0]

    def rows(other, shift):
        return pl.ds(pl.multiple_of(place(other, shift) * size, size), size)

    meet((up, down, across))
    started = []

    def push(number, target, source, other, shift, span):
        where = out.at[rows(other, shift), cols(span)]
        if source is None:
            source = where
        else:
            source = source.at[:, cols(span)]
        copy = pltpu.make_async_remote_copy(
            src_ref=source,
            dst_ref=where,
            send_sem=send.at[number],
            recv_sem=recv.at[number],
            device_id={"tensor": target},
            device_id_type=pl.DeviceIdType.MESH,
        )
        copy.start()
        started.append(copy)

    def arrived(number, other, shift, span):
        where = out.at[rows(other, shift), cols(span)]
        pltpu.make_async_remote_copy(
            src_ref=where,
            dst_ref=where,
            send_sem=send.at[number],
            recv_sem=recv.at[number],
            device_id={"tensor": up},
            device_id_type=pl.DeviceIdType.MESH,
        ).wait_recv()

    push(0, up, block, 0, 0, LOW)
    push(5, down, block, 0, 0, HIGH)
    push(10, across, block, 0, 0, HIGH)
    push(1, up, block, 0, 0, HIGH)
    push(6, down, block, 0, 0, LOW)
    push(11, across, block, 0, 0, LOW)
    own = pltpu.make_async_copy(block, out.at[rows(0, 0), :], own_sem)
    own.start()
    arrived(0, 0, -1, LOW)
    push(2, up, None, 0, -1, LOW)
    push(12, across, None, 0, -1, LOW)
    arrived(5, 0, 1, HIGH)
    push(7, down, None, 0, 1, HIGH)
    arrived(10, 1, 0, HIGH)
    push(3, up, None, 1, 0, HIGH)
    push(8, down, None, 1, 0, HIGH)
    arrived(6, 0, 1, LOW)
    push(13, across, None, 0, 1, LOW)
    arrived(12, 1, -1, LOW)
    push(4, up, None, 1, -1, (0, 2))
    arrived(7, 0, 2, HIGH)
    push(14, across, None, 0, 2, (4, 6))
    arrived(13, 1, 1, LOW)
    arrived(8, 1, 1, HIGH)
    push(9, down, None, 1, 1, (2, 4))
    arrived(1, 0, -1, HIGH)
    arrived(11, 1, 0, LOW)
    arrived(2, 0, 2, LOW)
    arrived(3, 1, -1, HIGH)
    arrived(4, 1, 2, (0, 2))
    arrived(9, 1, 2, (2, 4))
    arrived(14, 1, 2, (4, 6))
    for copy in started:
        copy.wait_send()
    own.wait()


def gather_rows(block):
    size, width = block.shape
    return pl.pallas_call(
        gather_kernel,
        out_shape=jax.ShapeDtypeStruct((8 * size, width), block.dtype),
        in_specs=[pl.BlockSpec(memory_space=pltpu.VMEM)],
        out_specs=pl.BlockSpec(memory_space=pltpu.VMEM),
        scratch_shapes=[
            pltpu.SemaphoreType.DMA((15,)),
            pltpu.SemaphoreType.DMA((15,)),
            pltpu.SemaphoreType.DMA(()),
        ],
        compiler_params=pltpu.CompilerParams(
            collective_id=0, has_side_effects=True, vmem_limit_bytes=40 << 20
        ),
        cost_estimate=pl.CostEstimate(
            flops=0, bytes_accessed=180 << 20, transcendentals=0
        ),
        name="gather_rows",
    )(block)


def scatter_kernel(partial, out, landing, staged, send, recv):
    place = ring_places()
    up, down, across = place(0, 1), place(0, -1), place(1, 0)
    size = out.shape[0]

    def rows(other, shift):
        return pl.ds(pl.multiple_of(place(other, shift) * size, size), size)

    meet((up, down, across))
    started = []

    def push(number, target, source, width):
        copy = pltpu.make_async_remote_copy(
            src_ref=source,
            dst_ref=landing.at[number, :, 0 : width * SIXTH],
            send_sem=send.at[number],
            recv_sem=recv.at[number],
            device_id={"tensor": target},
            device_id_type=pl.DeviceIdType.MESH,
        )
        copy.start()
        started.append(copy)

    def plain(number, target, other, shift, span):
        push(number, target, partial.at[rows(other, shift), cols(span)], span[1] - span[0])

    def arrived(number, width=3):
        where = landing.at[number, :, 0 : width * SIXTH]
        pltpu.make_async_remote_copy(
            src_ref=where,
            dst_ref=where,
            send_sem=send.at[number],
            recv_sem=recv.at[number],
            device_id={"tensor": up},
            device_id_type=pl.DeviceIdType.MESH,
        ).wait_recv()

    def summed(number, target, slot, other, shift, span, parts):
        for piece in range(span[0], span[1]):
            total = partial[rows(other, shift), cols((piece, piece + 1))].astype(jnp.float32)
            for landed, first, over in parts:
                if over[0] <= piece < over[1]:
                    total += landing[landed, :, cols((piece - first, piece - first + 1))].astype(jnp.float32)
            staged[slot, :, cols((piece - span[0], piece - span[0] + 1))] = total.astype(jnp.bfloat16)
        push(number, target, staged.at[slot], 3)

    plain(0, down, 1, 2, (0, 2))
    plain(5, up, 1, 2, (2, 4))
    plain(10, across, 1, 2, (4, 6))
    plain(1, down, 1, -1, HIGH)
    plain(2, down, 0, 2, LOW)
    plain(3, down, 0, -1, HIGH)
    arrived(5, 2)
    summed(6, up, 0, 1, 1, HIGH, ((5, 2, (2, 4)),))
    arrived(0, 2)
    summed(11, across, 1, 1, -1, LOW, ((0, 0, (0, 2)),))
    arrived(10, 2)
    summed(7, up, 2, 0, 2, HIGH, ((10, 4, (4, 6)),))
    summed(12, across, 3, 1, 1, LOW, ((5, 2, (2, 4)),))
    plain(13, across, 1, 0, LOW)
    arrived(2)
    arrived(11)
    summed(4, down, 4, 0, -1, LOW, ((2, 0, LOW), (11, 0, LOW)))
    arrived(12)
    summed(8, up, 5, 0, 1, LOW, ((12, 0, LOW),))
    arrived(7)
    summed(9, up, 6, 0, 1, HIGH, ((7, 3, HIGH),))
    arrived(1)
    arrived(6)
    summed(14, across, 7, 1, 0, HIGH, ((1, 3, HIGH), (6, 3, HIGH)))
    arrived(4)
    arrived(8)
    arrived(13)
    for piece in range(3):
        total = partial[rows(0, 0), cols((piece, piece + 1))].astype(jnp.float32)
        for landed in (4, 8, 13):
            total += landing[landed, :, cols((piece, piece + 1))].astype(jnp.float32)
        out[:, cols((piece, piece + 1))] = total
    arrived(3)
    arrived(9)
    arrived(14)
    for piece in range(3):
        total = partial[rows(0, 0), cols((piece + 3, piece + 4))].astype(jnp.float32)
        for landed in (3, 9, 14):
            total += landing[landed, :, cols((piece, piece + 1))].astype(jnp.float32)
        out[:, cols((piece + 3, piece + 4))] = total
    for copy in started:
        copy.wait_send()


def scatter_rows(partial, collective_id, name):
    height, width = partial.shape
    size = height // 8
    return pl.pallas_call(
        scatter_kernel,
        out_shape=jax.ShapeDtypeStruct((size, width), jnp.float32),
        in_specs=[pl.BlockSpec(memory_space=pltpu.VMEM)],
        out_specs=pl.BlockSpec(memory_space=pltpu.VMEM),
        scratch_shapes=[
            pltpu.VMEM((15, size, width // 2), jnp.bfloat16),
            pltpu.VMEM((8, size, width // 2), jnp.bfloat16),
            pltpu.SemaphoreType.DMA((15,)),
            pltpu.SemaphoreType.DMA((15,)),
        ],
        compiler_params=pltpu.CompilerParams(
            collective_id=collective_id, has_side_effects=True, vmem_limit_bytes=40 << 20
        ),
        cost_estimate=pl.CostEstimate(
            flops=0, bytes_accessed=180 << 20, transcendentals=0
        ),
        name=name,
    )(partial)


def on_device(
    activations, mod_gain, mod_shift, out_gate, qkv_weight, out_weight, tile_mask, cotangent
):
    shard_rows = activations.shape[0]
    frame_count = tile_mask.shape[0]
    standard, inverse, modulated = norm_rows(activations, mod_gain, mod_shift)
    rows_here = gather_rows(modulated)
    weight = jnp.transpose(qkv_weight, (1, 0, 2))
    joined = jnp.einsum("rd,hdc->hrc", rows_here, weight, preferred_element_type=jnp.float32)
    joined = joined.astype(jnp.bfloat16)
    count = lax.axis_size("tm")
    scaled = (cotangent.astype(jnp.float32) * out_gate).astype(jnp.bfloat16)
    grad_out = jnp.einsum("rd,hcd->hrc", scaled, out_weight, preferred_element_type=jnp.float32)
    grad_out = grad_out.astype(jnp.bfloat16)
    bias = mask_bias(tile_mask, lax.axis_index("tm") * frame_count, frame_count * count)
    output, grad_queries, grad_pairs = attention(joined, grad_out, bias)
    projected = jnp.einsum("hrc,hcd->rd", output, out_weight, preferred_element_type=jnp.float32)
    projection = scatter_rows(projected.astype(jnp.bfloat16), 1, "scatter_out")
    layer_out = (activations.astype(jnp.float32) + out_gate * projection).astype(jnp.bfloat16)
    grad_joined = jnp.concatenate([grad_queries, grad_pairs], axis=-1)
    grad_rows = jnp.einsum("hrc,hdc->rd", grad_joined, weight, preferred_element_type=jnp.float32)
    grad_norm = scatter_rows(grad_rows.astype(jnp.bfloat16), 2, "scatter_grad")
    own_cotangent = lax.dynamic_slice_in_dim(
        cotangent, lax.axis_index("tensor") * shard_rows, shard_rows, 0
    )
    input_grad = norm_back(grad_norm, standard, inverse, mod_gain, own_cotangent)
    return (layer_out, input_grad)


def solution(mesh):
    placed = (
        P(("tm", "tensor"), None),
        P(),
        P(),
        P(),
        P(None, "tensor", None),
        P("tensor", None, None),
        P("tm", None, None, None),
        P("tm", None),
    )
    return jax.shard_map(
        on_device,
        mesh=mesh,
        in_specs=placed,
        out_specs=(P(("tm", "tensor"), None), P(("tm", "tensor"), None)),
        check_vma=False,
    )
```

```python
import functools
import math

import jax
import jax.numpy as jnp
from jax import lax
from jax.experimental import pallas as pl
from jax.experimental.pallas import tpu as pltpu
from jax.sharding import PartitionSpec as P

FRAME = 256
TILE = 64
RADIUS = 3
SPAN = 2 * RADIUS + 1
HD = 128
EPSILON = 1e-06
MASKED = -1e30
HELD = 3


def norm_rows(inputs, mod_gain, mod_shift):
    floated = inputs.astype(jnp.float32)
    row_mean = jnp.mean(floated, axis=-1, keepdims=True)
    centered = floated - row_mean
    inverse = lax.rsqrt(jnp.mean(centered * centered, axis=-1, keepdims=True) + EPSILON)
    standard = centered * inverse
    return (standard, inverse, (standard * mod_gain + mod_shift).astype(jnp.bfloat16))


def norm_back(grad_norm, standard, inverse, mod_gain, cotangent):
    scaled_grad = grad_norm * mod_gain
    centered = scaled_grad - jnp.mean(scaled_grad, axis=-1, keepdims=True)
    projected = standard * jnp.mean(scaled_grad * standard, axis=-1, keepdims=True)
    return (cotangent.astype(jnp.float32) + inverse * (centered - projected)).astype(jnp.bfloat16)


def mask_bias(tile_mask, first_frame, total_frames):
    frames = lax.broadcasted_iota(jnp.int32, tile_mask.shape, 0) + first_frame
    offsets = lax.broadcasted_iota(jnp.int32, tile_mask.shape, 1)
    query_tile = lax.broadcasted_iota(jnp.int32, tile_mask.shape, 2)
    key_tile = lax.broadcasted_iota(jnp.int32, tile_mask.shape, 3)
    source = frames + offsets - RADIUS
    diagonal = (offsets == RADIUS) & (query_tile == key_tile)
    allowed = ((tile_mask == 1) | diagonal) & (source >= 0) & (source < total_frames)
    bias = jnp.where(allowed, 0.0, MASKED).astype(jnp.float32)
    return jnp.transpose(bias, (0, 1, 3, 2)).reshape(-1)


def dot(a, b, dims):
    return lax.dot_general(a, b, (dims, ((), ())), preferred_element_type=jnp.float32)


NN = ((1,), (0,))
NT = ((1,), (1,))


def attention_kernel(
    bias, joined, grad_out, out, grad_q, grad_pairs,
    keys, values, keys_t, values_t, exps, grad_k, grad_v, own, halo, rims, landed,
    halo_send, halo_recv, rims_send, rims_recv,
):
    head = pl.program_id(0)
    frame = pl.program_id(1)
    heads = pl.num_programs(0)
    frames = pl.num_programs(1)
    block = 4 * FRAME
    rim = RADIUS * FRAME
    spare = block - rim
    scale = HD ** (-0.5)
    me = lax.axis_index("tm")
    count = lax.axis_size("tm")
    above, below = lax.rem(me + 1, count), lax.rem(me + count - 1, count)

    def halo_copy(which, side):
        rows = slice(spare, block) if side == 0 else slice(0, rim)
        return pltpu.make_async_remote_copy(
            src_ref=joined.at[which, rows, HD : 3 * HD],
            dst_ref=halo.at[which, side],
            send_sem=halo_send.at[which, side],
            recv_sem=halo_recv.at[which, side],
            device_id={"tm": above if side == 0 else below},
            device_id_type=pl.DeviceIdType.MESH,
        )

    def rims_copy(which, side):
        return pltpu.make_async_remote_copy(
            src_ref=rims.at[which, side],
            dst_ref=landed.at[which, side],
            send_sem=rims_send.at[which, side],
            recv_sem=rims_recv.at[which, side],
            device_id={"tm": above if side == 0 else below},
            device_id_type=pl.DeviceIdType.MESH,
        )

    @pl.when((head == 0) & (frame == 0))
    def _():
        barrier = pltpu.get_barrier_semaphore()
        for neighbour in (above, below):
            pl.semaphore_signal(
                barrier, inc=1, device_id={"tm": neighbour}, device_id_type=pl.DeviceIdType.MESH
            )
        pl.semaphore_wait(barrier, 2)
        for which in range(HELD):
            for side in range(2):
                halo_copy(which, side).start()

    @pl.when(frame == 0)
    def _():
        keys[rim : rim + block, :] = joined[head, :, HD : 2 * HD]
        values[rim : rim + block, :] = joined[head, :, 2 * HD :]
        grad_k[...] = jnp.zeros_like(grad_k)
        grad_v[...] = jnp.zeros_like(grad_v)
        for which in range(HELD):

            @pl.when(head == which)
            def _():
                for side in range(2):
                    halo_copy(which, side).wait_recv()
                keys[0:rim, :] = halo[which, 0, :, 0:HD]
                keys[rim + block :, :] = halo[which, 1, :, 0:HD]
                values[0:rim, :] = halo[which, 0, :, HD:]
                values[rim + block :, :] = halo[which, 1, :, HD:]

        for part in range(block // FRAME + 2 * RADIUS):
            rows = slice(part * FRAME, (part + 1) * FRAME)
            keys_t[part, :, :] = keys[rows, :].T
            values_t[part, :, :] = values[rows, :].T

    query_tile = lax.broadcasted_iota(jnp.int32, (1, FRAME), 1) // TILE

    def bias_line(offset, tile):
        first = (frame * SPAN + offset) * 16 + tile * 4
        line = jnp.full((1, FRAME), bias[first], jnp.float32)
        for other in range(1, 4):
            line = jnp.where(query_tile == other, bias[first + other], line)
        return line

    own_rows = pl.ds(pl.multiple_of(frame * FRAME, FRAME), FRAME)
    query = joined[head, own_rows, 0:HD]
    grads = grad_out[0, own_rows, :]

    totals = jnp.zeros((8, FRAME), jnp.float32)
    numer = jnp.zeros((HD, FRAME), jnp.float32)
    for offset in range(SPAN):
        rows = pl.ds(pl.multiple_of((frame + offset) * FRAME, FRAME), FRAME)
        scores = dot(keys[rows, :], query, NT) * (scale * math.log2(math.e))
        parts = []
        for tile in range(FRAME // TILE):
            line = bias_line(offset, tile)
            parts.append(jnp.exp2(scores[tile * TILE : (tile + 1) * TILE, :] + line))
        exponent = jnp.concatenate(parts, axis=0)
        exps[offset * FRAME : (offset + 1) * FRAME, :] = exponent
        totals += jnp.sum(exponent.reshape(FRAME // 8, 8, FRAME), axis=0)
        numer += dot(values_t[frame + offset], exponent.astype(jnp.bfloat16), NN)
    inverse = 1.0 / jnp.sum(totals, axis=0, keepdims=True)
    output = (numer * inverse).T.astype(jnp.bfloat16)
    out[0] = output
    product = grads.astype(jnp.float32) * output.astype(jnp.float32)
    delta = jnp.sum(product.T, axis=0, keepdims=True)

    grad_query = jnp.zeros((HD, FRAME), jnp.float32)
    for offset in range(SPAN):
        rows = pl.ds(pl.multiple_of((frame + offset) * FRAME, FRAME), FRAME)
        probability = exps[offset * FRAME : (offset + 1) * FRAME, :] * inverse
        grad_probs = dot(values[rows, :], grads, NT)
        grad_v[rows, :] += dot(probability.astype(jnp.bfloat16), grads, NN)
        grad_scores = (probability * (grad_probs - delta)).astype(jnp.bfloat16)
        grad_k[rows, :] += dot(grad_scores, query, NN)
        grad_query += dot(keys_t[frame + offset], grad_scores, NN)
    grad_q[0] = (grad_query * scale).T.astype(jnp.bfloat16)

    @pl.when(frame == frames - 1)
    def _():
        for which in range(HELD):

            @pl.when(head == which)
            def _():
                own[which, :, 0:HD] = grad_k[rim : rim + block, :] * scale
                own[which, :, HD:] = grad_v[rim : rim + block, :]
                rims[which, 1, :, 0:HD] = (grad_k[0:rim, :] * scale).astype(jnp.bfloat16)
                rims[which, 0, :, 0:HD] = (grad_k[rim + block :, :] * scale).astype(jnp.bfloat16)
                rims[which, 1, :, HD:] = grad_v[0:rim, :].astype(jnp.bfloat16)
                rims[which, 0, :, HD:] = grad_v[rim + block :, :].astype(jnp.bfloat16)
                for side in range(2):
                    rims_copy(which, side).start()

    @pl.when((head == heads - 1) & (frame == frames - 1))
    def _():
        for which in range(HELD):
            for side in range(2):
                rims_copy(which, side).wait_recv()
            own[which, 0:rim, :] += landed[which, 0].astype(jnp.float32)
            own[which, spare:, :] += landed[which, 1].astype(jnp.float32)
            grad_pairs[which, :, :] = own[which, :, :].astype(jnp.bfloat16)
        for which in range(HELD):
            for side in range(2):
                halo_copy(which, side).wait_send()
                rims_copy(which, side).wait_send()


def attention(joined, grad_out, bias):
    heads, block, _ = joined.shape
    frames = block // FRAME
    rim = RADIUS * FRAME
    whole = block + 2 * rim
    per_head = lambda head, frame: (head, 0, 0)
    per_frame = lambda head, frame: (head, frame, 0)
    constant = lambda head, frame: (0, 0, 0)
    return pl.pallas_call(
        attention_kernel,
        grid=(heads, frames),
        out_shape=(
            jax.ShapeDtypeStruct((heads, block, HD), jnp.bfloat16),
            jax.ShapeDtypeStruct((heads, block, HD), jnp.bfloat16),
            jax.ShapeDtypeStruct((heads, block, 2 * HD), jnp.bfloat16),
        ),
        in_specs=[
            pl.BlockSpec(memory_space=pltpu.SMEM),
            pl.BlockSpec((heads, block, 3 * HD), constant),
            pl.BlockSpec((1, block, HD), per_head),
        ],
        out_specs=(
            pl.BlockSpec((1, FRAME, HD), per_frame),
            pl.BlockSpec((1, FRAME, HD), per_frame),
            pl.BlockSpec((heads, block, 2 * HD), constant),
        ),
        scratch_shapes=[
            pltpu.VMEM((whole, HD), jnp.bfloat16),
            pltpu.VMEM((whole, HD), jnp.bfloat16),
            pltpu.VMEM((whole // FRAME, HD, FRAME), jnp.bfloat16),
            pltpu.VMEM((whole // FRAME, HD, FRAME), jnp.bfloat16),
            pltpu.VMEM((SPAN * FRAME, FRAME), jnp.float32),
            pltpu.VMEM((whole, HD), jnp.float32),
            pltpu.VMEM((whole, HD), jnp.float32),
            pltpu.VMEM((heads, block, 2 * HD), jnp.float32),
            pltpu.VMEM((heads, 2, rim, 2 * HD), jnp.bfloat16),
            pltpu.VMEM((heads, 2, rim, 2 * HD), jnp.bfloat16),
            pltpu.VMEM((heads, 2, rim, 2 * HD), jnp.bfloat16),
            pltpu.SemaphoreType.DMA((heads, 2)),
            pltpu.SemaphoreType.DMA((heads, 2)),
            pltpu.SemaphoreType.DMA((heads, 2)),
            pltpu.SemaphoreType.DMA((heads, 2)),
        ],
        compiler_params=pltpu.CompilerParams(
            dimension_semantics=("arbitrary", "arbitrary"),
            collective_id=3,
            has_side_effects=True,
            vmem_limit_bytes=40 << 20,
        ),
        name="attention",
    )(bias, joined, grad_out)


SIXTH = 512
LOW = (0, 3)
HIGH = (3, 6)


def cols(span):
    return slice(span[0] * SIXTH, span[1] * SIXTH)


def ring_places():
    me = lax.axis_index("tensor")
    z, x = me // 4, me % 4

    def place(other, shift):
        return ((z + other) % 2) * 4 + (x + shift) % 4

    return place


def meet(neighbours):
    barrier = pltpu.get_barrier_semaphore()
    for neighbour in neighbours:
        pl.semaphore_signal(
            barrier, inc=1, device_id={"tensor": neighbour}, device_id_type=pl.DeviceIdType.MESH
        )
    pl.semaphore_wait(barrier, len(neighbours))


def gather_kernel(
    gate, block, cotangent, weight, out_weight, joined, grad_out,
    out, held_cotangent, held_weight, held_out_weight, send, recv, own_sem, loads,
):
    fetches = []
    for number, (source, target) in enumerate(
        ((cotangent, held_cotangent), (out_weight, held_out_weight), (weight, held_weight))
    ):
        fetches.append(pltpu.make_async_copy(source, target, loads.at[number]))
        fetches[-1].start()
    place = ring_places()
    up, down, across = place(0, 1), place(0, -1), place(1, 0)
    size = block.shape[0]

    def rows(other, shift):
        return pl.ds(pl.multiple_of(place(other, shift) * size, size), size)

    meet((up, down, across))
    started = []

    def push(number, target, source, other, shift, span):
        where = out.at[rows(other, shift), cols(span)]
        if source is None:
            source = where
        else:
            source = source.at[:, cols(span)]
        copy = pltpu.make_async_remote_copy(
            src_ref=source,
            dst_ref=where,
            send_sem=send.at[number],
            recv_sem=recv.at[number],
            device_id={"tensor": target},
            device_id_type=pl.DeviceIdType.MESH,
        )
        copy.start()
        started.append(copy)

    def arrived(number, other, shift, span):
        where = out.at[rows(other, shift), cols(span)]
        pltpu.make_async_remote_copy(
            src_ref=where,
            dst_ref=where,
            send_sem=send.at[number],
            recv_sem=recv.at[number],
            device_id={"tensor": up},
            device_id_type=pl.DeviceIdType.MESH,
        ).wait_recv()

    push(0, up, block, 0, 0, LOW)
    push(5, down, block, 0, 0, HIGH)
    push(10, across, block, 0, 0, HIGH)
    push(1, up, block, 0, 0, HIGH)
    push(6, down, block, 0, 0, LOW)
    push(11, across, block, 0, 0, LOW)
    own = pltpu.make_async_copy(block, out.at[rows(0, 0), :], own_sem)
    own.start()
    fetches[0].wait()
    fetches[1].wait()

    def grad_rows(step, carry):
        chunk = pl.ds(pl.multiple_of(step * FRAME, FRAME), FRAME)
        scaled = (held_cotangent[chunk, :].astype(jnp.float32) * gate[...]).astype(jnp.bfloat16)
        for head in range(HELD):
            grad_out[head, chunk, :] = dot(scaled, held_out_weight[head], NT).astype(jnp.bfloat16)
        return carry

    lax.fori_loop(0, 8 * size // FRAME, grad_rows, 0)

    def join(other, shift):
        for head in range(HELD):
            product = dot(out[rows(other, shift), :], held_weight[head], NN)
            joined[head, rows(other, shift), :] = product.astype(jnp.bfloat16)

    arrived(0, 0, -1, LOW)
    push(2, up, None, 0, -1, LOW)
    push(12, across, None, 0, -1, LOW)
    arrived(5, 0, 1, HIGH)
    push(7, down, None, 0, 1, HIGH)
    arrived(10, 1, 0, HIGH)
    push(3, up, None, 1, 0, HIGH)
    push(8, down, None, 1, 0, HIGH)
    own.wait()
    fetches[2].wait()
    join(0, 0)
    arrived(6, 0, 1, LOW)
    push(13, across, None, 0, 1, LOW)
    arrived(1, 0, -1, HIGH)
    join(0, -1)
    join(0, 1)
    arrived(11, 1, 0, LOW)
    join(1, 0)
    arrived(12, 1, -1, LOW)
    push(4, up, None, 1, -1, (0, 2))
    arrived(7, 0, 2, HIGH)
    push(14, across, None, 0, 2, (4, 6))
    arrived(13, 1, 1, LOW)
    arrived(8, 1, 1, HIGH)
    push(9, down, None, 1, 1, (2, 4))
    join(1, 1)
    arrived(2, 0, 2, LOW)
    join(0, 2)
    arrived(3, 1, -1, HIGH)
    join(1, -1)
    arrived(4, 1, 2, (0, 2))
    arrived(9, 1, 2, (2, 4))
    arrived(14, 1, 2, (4, 6))
    join(1, 2)
    for copy in started:
        copy.wait_send()


def gather_rows(gate, block, cotangent, weight, out_weight):
    size, width = block.shape
    in_vmem = pl.BlockSpec(memory_space=pltpu.VMEM)
    anywhere = pl.BlockSpec(memory_space=pl.ANY)
    return pl.pallas_call(
        gather_kernel,
        out_shape=(
            jax.ShapeDtypeStruct((HELD, 8 * size, 3 * HD), block.dtype),
            jax.ShapeDtypeStruct((HELD, 8 * size, HD), block.dtype),
        ),
        in_specs=[in_vmem, in_vmem, anywhere, anywhere, anywhere],
        out_specs=(in_vmem, in_vmem),
        scratch_shapes=[
            pltpu.VMEM((8 * size, width), block.dtype),
            pltpu.VMEM(cotangent.shape, cotangent.dtype),
            pltpu.VMEM(weight.shape, weight.dtype),
            pltpu.VMEM(out_weight.shape, out_weight.dtype),
            pltpu.SemaphoreType.DMA((15,)),
            pltpu.SemaphoreType.DMA((15,)),
            pltpu.SemaphoreType.DMA(()),
            pltpu.SemaphoreType.DMA((3,)),
        ],
        compiler_params=pltpu.CompilerParams(
            collective_id=0, has_side_effects=True, vmem_limit_bytes=48 << 20
        ),
        name="gather_rows",
    )(gate.reshape(1, width), block, cotangent, weight, out_weight)


def scatter_kernel(partial, out, landing, staged, send, recv):
    place = ring_places()
    up, down, across = place(0, 1), place(0, -1), place(1, 0)
    size = out.shape[0]

    def rows(other, shift):
        return pl.ds(pl.multiple_of(place(other, shift) * size, size), size)

    meet((up, down, across))
    started = []

    def push(number, target, source, width):
        copy = pltpu.make_async_remote_copy(
            src_ref=source,
            dst_ref=landing.at[number, :, 0 : width * SIXTH],
            send_sem=send.at[number],
            recv_sem=recv.at[number],
            device_id={"tensor": target},
            device_id_type=pl.DeviceIdType.MESH,
        )
        copy.start()
        started.append(copy)

    def plain(number, target, other, shift, span):
        push(number, target, partial.at[rows(other, shift), cols(span)], span[1] - span[0])

    def arrived(number, width=3):
        where = landing.at[number, :, 0 : width * SIXTH]
        pltpu.make_async_remote_copy(
            src_ref=where,
            dst_ref=where,
            send_sem=send.at[number],
            recv_sem=recv.at[number],
            device_id={"tensor": up},
            device_id_type=pl.DeviceIdType.MESH,
        ).wait_recv()

    def summed(number, target, slot, other, shift, span, parts):
        for piece in range(span[0], span[1]):
            total = partial[rows(other, shift), cols((piece, piece + 1))].astype(jnp.float32)
            for landed, first, over in parts:
                if over[0] <= piece < over[1]:
                    total += landing[landed, :, cols((piece - first, piece - first + 1))].astype(jnp.float32)
            staged[slot, :, cols((piece - span[0], piece - span[0] + 1))] = total.astype(jnp.bfloat16)
        push(number, target, staged.at[slot], 3)

    plain(0, down, 1, 2, (0, 2))
    plain(5, up, 1, 2, (2, 4))
    plain(10, across, 1, 2, (4, 6))
    plain(1, down, 1, -1, HIGH)
    plain(2, down, 0, 2, LOW)
    plain(3, down, 0, -1, HIGH)
    arrived(5, 2)
    summed(6, up, 0, 1, 1, HIGH, ((5, 2, (2, 4)),))
    arrived(0, 2)
    summed(11, across, 1, 1, -1, LOW, ((0, 0, (0, 2)),))
    arrived(10, 2)
    summed(7, up, 2, 0, 2, HIGH, ((10, 4, (4, 6)),))
    summed(12, across, 3, 1, 1, LOW, ((5, 2, (2, 4)),))
    plain(13, across, 1, 0, LOW)
    arrived(2)
    arrived(11)
    summed(4, down, 4, 0, -1, LOW, ((2, 0, LOW), (11, 0, LOW)))
    arrived(12)
    summed(8, up, 5, 0, 1, LOW, ((12, 0, LOW),))
    arrived(7)
    summed(9, up, 6, 0, 1, HIGH, ((7, 3, HIGH),))
    arrived(1)
    arrived(6)
    summed(14, across, 7, 1, 0, HIGH, ((1, 3, HIGH), (6, 3, HIGH)))
    arrived(4)
    arrived(8)
    arrived(13)
    for piece in range(3):
        total = partial[rows(0, 0), cols((piece, piece + 1))].astype(jnp.float32)
        for landed in (4, 8, 13):
            total += landing[landed, :, cols((piece, piece + 1))].astype(jnp.float32)
        out[:, cols((piece, piece + 1))] = total
    arrived(3)
    arrived(9)
    arrived(14)
    for piece in range(3):
        total = partial[rows(0, 0), cols((piece + 3, piece + 4))].astype(jnp.float32)
        for landed in (3, 9, 14):
            total += landing[landed, :, cols((piece, piece + 1))].astype(jnp.float32)
        out[:, cols((piece + 3, piece + 4))] = total
    for copy in started:
        copy.wait_send()


def scatter_rows(partial, collective_id, name):
    height, width = partial.shape
    size = height // 8
    return pl.pallas_call(
        scatter_kernel,
        out_shape=jax.ShapeDtypeStruct((size, width), jnp.float32),
        in_specs=[pl.BlockSpec(memory_space=pltpu.VMEM)],
        out_specs=pl.BlockSpec(memory_space=pltpu.VMEM),
        scratch_shapes=[
            pltpu.VMEM((15, size, width // 2), jnp.bfloat16),
            pltpu.VMEM((8, size, width // 2), jnp.bfloat16),
            pltpu.SemaphoreType.DMA((15,)),
            pltpu.SemaphoreType.DMA((15,)),
        ],
        compiler_params=pltpu.CompilerParams(
            collective_id=collective_id, has_side_effects=True, vmem_limit_bytes=40 << 20
        ),
        cost_estimate=pl.CostEstimate(
            flops=0, bytes_accessed=180 << 20, transcendentals=0
        ),
        name=name,
    )(partial)


def on_device(
    activations, mod_gain, mod_shift, out_gate, qkv_weight, out_weight, tile_mask, cotangent
):
    shard_rows = activations.shape[0]
    frame_count = tile_mask.shape[0]
    standard, inverse, modulated = norm_rows(activations, mod_gain, mod_shift)
    weight = jnp.transpose(qkv_weight, (1, 0, 2))
    joined, grad_out = gather_rows(out_gate, modulated, cotangent, weight, out_weight)
    count = lax.axis_size("tm")
    bias = mask_bias(tile_mask, lax.axis_index("tm") * frame_count, frame_count * count)
    output, grad_queries, grad_pairs = attention(joined, grad_out, bias)
    projected = jnp.einsum("hrc,hcd->rd", output, out_weight, preferred_element_type=jnp.float32)
    projection = scatter_rows(projected.astype(jnp.bfloat16), 1, "scatter_out")
    layer_out = (activations.astype(jnp.float32) + out_gate * projection).astype(jnp.bfloat16)
    grad_joined = jnp.concatenate([grad_queries, grad_pairs], axis=-1)
    grad_rows = jnp.einsum("hrc,hdc->rd", grad_joined, weight, preferred_element_type=jnp.float32)
    grad_norm = scatter_rows(grad_rows.astype(jnp.bfloat16), 2, "scatter_grad")
    own_cotangent = lax.dynamic_slice_in_dim(
        cotangent, lax.axis_index("tensor") * shard_rows, shard_rows, 0
    )
    input_grad = norm_back(grad_norm, standard, inverse, mod_gain, own_cotangent)
    return (layer_out, input_grad)


def solution(mesh):
    placed = (
        P(("tm", "tensor"), None),
        P(),
        P(),
        P(),
        P(None, "tensor", None),
        P("tensor", None, None),
        P("tm", None, None, None),
        P("tm", None),
    )
    return jax.shard_map(
        on_device,
        mesh=mesh,
        in_specs=placed,
        out_specs=(P(("tm", "tensor"), None), P(("tm", "tensor"), None)),
        check_vma=False,
    )
```

```python
import functools
import math

import jax
import jax.numpy as jnp
from jax import lax
from jax.experimental import pallas as pl
from jax.experimental.pallas import tpu as pltpu
from jax.sharding import PartitionSpec as P

FRAME = 256
TILE = 64
RADIUS = 3
SPAN = 2 * RADIUS + 1
HD = 128
EPSILON = 1e-06
MASKED = -1e30
HELD = 3


def norm_rows(inputs, mod_gain, mod_shift):
    floated = inputs.astype(jnp.float32)
    row_mean = jnp.mean(floated, axis=-1, keepdims=True)
    centered = floated - row_mean
    inverse = lax.rsqrt(jnp.mean(centered * centered, axis=-1, keepdims=True) + EPSILON)
    standard = centered * inverse
    return (standard, inverse, (standard * mod_gain + mod_shift).astype(jnp.bfloat16))


def norm_back(grad_norm, standard, inverse, mod_gain, cotangent):
    scaled_grad = grad_norm * mod_gain
    centered = scaled_grad - jnp.mean(scaled_grad, axis=-1, keepdims=True)
    projected = standard * jnp.mean(scaled_grad * standard, axis=-1, keepdims=True)
    return (cotangent.astype(jnp.float32) + inverse * (centered - projected)).astype(jnp.bfloat16)


def mask_bias(tile_mask, first_frame, total_frames):
    frames = lax.broadcasted_iota(jnp.int32, tile_mask.shape, 0) + first_frame
    offsets = lax.broadcasted_iota(jnp.int32, tile_mask.shape, 1)
    query_tile = lax.broadcasted_iota(jnp.int32, tile_mask.shape, 2)
    key_tile = lax.broadcasted_iota(jnp.int32, tile_mask.shape, 3)
    source = frames + offsets - RADIUS
    diagonal = (offsets == RADIUS) & (query_tile == key_tile)
    allowed = ((tile_mask == 1) | diagonal) & (source >= 0) & (source < total_frames)
    bias = jnp.where(allowed, 0.0, MASKED).astype(jnp.float32)
    return jnp.transpose(bias, (0, 1, 3, 2)).reshape(-1)


def dot(a, b, dims):
    return lax.dot_general(a, b, (dims, ((), ())), preferred_element_type=jnp.float32)


NN = ((1,), (0,))
NT = ((1,), (1,))


def attention_kernel(
    bias, joined, grad_out, out_weight, projected, grad_q, grad_pairs, out,
    keys, values, keys_t, values_t, exps, grad_k, grad_v, own, halo, rims, landed,
    halo_send, halo_recv, rims_send, rims_recv,
):
    head = pl.program_id(0)
    frame = pl.program_id(1)
    heads = pl.num_programs(0)
    frames = pl.num_programs(1)
    block = 4 * FRAME
    rim = RADIUS * FRAME
    spare = block - rim
    scale = HD ** (-0.5)
    me = lax.axis_index("tm")
    count = lax.axis_size("tm")
    above, below = lax.rem(me + 1, count), lax.rem(me + count - 1, count)

    def halo_copy(which, side):
        rows = slice(spare, block) if side == 0 else slice(0, rim)
        return pltpu.make_async_remote_copy(
            src_ref=joined.at[which, rows, HD : 3 * HD],
            dst_ref=halo.at[which, side],
            send_sem=halo_send.at[which, side],
            recv_sem=halo_recv.at[which, side],
            device_id={"tm": above if side == 0 else below},
            device_id_type=pl.DeviceIdType.MESH,
        )

    def rims_copy(which, side):
        return pltpu.make_async_remote_copy(
            src_ref=rims.at[which, side],
            dst_ref=landed.at[which, side],
            send_sem=rims_send.at[which, side],
            recv_sem=rims_recv.at[which, side],
            device_id={"tm": above if side == 0 else below},
            device_id_type=pl.DeviceIdType.MESH,
        )

    @pl.when((head == 0) & (frame == 0))
    def _():
        barrier = pltpu.get_barrier_semaphore()
        for neighbour in (above, below):
            pl.semaphore_signal(
                barrier, inc=1, device_id={"tm": neighbour}, device_id_type=pl.DeviceIdType.MESH
            )
        pl.semaphore_wait(barrier, 2)
        for which in range(HELD):
            for side in range(2):
                halo_copy(which, side).start()

    @pl.when(frame == 0)
    def _():
        keys[rim : rim + block, :] = joined[head, :, HD : 2 * HD]
        values[rim : rim + block, :] = joined[head, :, 2 * HD :]
        grad_k[...] = jnp.zeros_like(grad_k)
        grad_v[...] = jnp.zeros_like(grad_v)
        for which in range(HELD):

            @pl.when(head == which)
            def _():
                for side in range(2):
                    halo_copy(which, side).wait_recv()
                keys[0:rim, :] = halo[which, 0, :, 0:HD]
                keys[rim + block :, :] = halo[which, 1, :, 0:HD]
                values[0:rim, :] = halo[which, 0, :, HD:]
                values[rim + block :, :] = halo[which, 1, :, HD:]

        for part in range(block // FRAME + 2 * RADIUS):
            rows = slice(part * FRAME, (part + 1) * FRAME)
            keys_t[part, :, :] = keys[rows, :].T
            values_t[part, :, :] = values[rows, :].T

    query_tile = lax.broadcasted_iota(jnp.int32, (1, FRAME), 1) // TILE

    def bias_line(offset, tile):
        first = (frame * SPAN + offset) * 16 + tile * 4
        line = jnp.full((1, FRAME), bias[first], jnp.float32)
        for other in range(1, 4):
            line = jnp.where(query_tile == other, bias[first + other], line)
        return line

    own_rows = pl.ds(pl.multiple_of(frame * FRAME, FRAME), FRAME)
    query = joined[head, own_rows, 0:HD]
    grads = grad_out[0, own_rows, :]

    totals = jnp.zeros((8, FRAME), jnp.float32)
    numer = jnp.zeros((HD, FRAME), jnp.float32)
    for offset in range(SPAN):
        rows = pl.ds(pl.multiple_of((frame + offset) * FRAME, FRAME), FRAME)
        scores = dot(keys[rows, :], query, NT) * (scale * math.log2(math.e))
        parts = []
        for tile in range(FRAME // TILE):
            line = bias_line(offset, tile)
            parts.append(jnp.exp2(scores[tile * TILE : (tile + 1) * TILE, :] + line))
        exponent = jnp.concatenate(parts, axis=0)
        exps[offset * FRAME : (offset + 1) * FRAME, :] = exponent
        totals += jnp.sum(exponent.reshape(FRAME // 8, 8, FRAME), axis=0)
        numer += dot(values_t[frame + offset], exponent.astype(jnp.bfloat16), NN)
    inverse = 1.0 / jnp.sum(totals, axis=0, keepdims=True)
    output = (numer * inverse).T.astype(jnp.bfloat16)
    out[head, own_rows, :] = output
    product = grads.astype(jnp.float32) * output.astype(jnp.float32)
    delta = jnp.sum(product.T, axis=0, keepdims=True)

    grad_query = jnp.zeros((HD, FRAME), jnp.float32)
    for offset in range(SPAN):
        rows = pl.ds(pl.multiple_of((frame + offset) * FRAME, FRAME), FRAME)
        probability = exps[offset * FRAME : (offset + 1) * FRAME, :] * inverse
        grad_probs = dot(values[rows, :], grads, NT)
        grad_v[rows, :] += dot(probability.astype(jnp.bfloat16), grads, NN)
        grad_scores = (probability * (grad_probs - delta)).astype(jnp.bfloat16)
        grad_k[rows, :] += dot(grad_scores, query, NN)
        grad_query += dot(keys_t[frame + offset], grad_scores, NN)
    grad_q[0] = (grad_query * scale).T.astype(jnp.bfloat16)

    @pl.when(frame == frames - 1)
    def _():
        for which in range(HELD):

            @pl.when(head == which)
            def _():
                own[which, :, 0:HD] = grad_k[rim : rim + block, :] * scale
                own[which, :, HD:] = grad_v[rim : rim + block, :]
                rims[which, 1, :, 0:HD] = (grad_k[0:rim, :] * scale).astype(jnp.bfloat16)
                rims[which, 0, :, 0:HD] = (grad_k[rim + block :, :] * scale).astype(jnp.bfloat16)
                rims[which, 1, :, HD:] = grad_v[0:rim, :].astype(jnp.bfloat16)
                rims[which, 0, :, HD:] = grad_v[rim + block :, :].astype(jnp.bfloat16)
                for side in range(2):
                    rims_copy(which, side).start()

    @pl.when((head == heads - 1) & (frame == frames - 1))
    def _():
        def project(step, carry):
            chunk = pl.ds(pl.multiple_of(step * FRAME, FRAME), FRAME)
            joint = jnp.concatenate([out[which, chunk, :] for which in range(HELD)], axis=1)
            projected[chunk, :] = dot(joint, out_weight[...], NN).astype(jnp.bfloat16)
            return carry

        lax.fori_loop(0, block // FRAME, project, 0)
        for which in range(HELD):
            for side in range(2):
                rims_copy(which, side).wait_recv()
            own[which, 0:rim, :] += landed[which, 0].astype(jnp.float32)
            own[which, spare:, :] += landed[which, 1].astype(jnp.float32)
            grad_pairs[which, :, :] = own[which, :, :].astype(jnp.bfloat16)
        for which in range(HELD):
            for side in range(2):
                halo_copy(which, side).wait_send()
                rims_copy(which, side).wait_send()


def attention(joined, grad_out, bias, out_weight):
    heads, block, _ = joined.shape
    frames = block // FRAME
    rim = RADIUS * FRAME
    whole = block + 2 * rim
    per_head = lambda head, frame: (head, 0, 0)
    per_frame = lambda head, frame: (head, frame, 0)
    constant = lambda head, frame: (0, 0, 0)
    return pl.pallas_call(
        attention_kernel,
        grid=(heads, frames),
        out_shape=(
            jax.ShapeDtypeStruct((block, out_weight.shape[1]), jnp.bfloat16),
            jax.ShapeDtypeStruct((heads, block, HD), jnp.bfloat16),
            jax.ShapeDtypeStruct((heads, block, 2 * HD), jnp.bfloat16),
        ),
        in_specs=[
            pl.BlockSpec(memory_space=pltpu.SMEM),
            pl.BlockSpec((heads, block, 3 * HD), constant),
            pl.BlockSpec((1, block, HD), per_head),
            pl.BlockSpec(out_weight.shape, lambda head, frame: (0, 0)),
        ],
        out_specs=(
            pl.BlockSpec((block, out_weight.shape[1]), lambda head, frame: (0, 0)),
            pl.BlockSpec((1, FRAME, HD), per_frame),
            pl.BlockSpec((heads, block, 2 * HD), constant),
        ),
        scratch_shapes=[
            pltpu.VMEM((heads, block, HD), jnp.bfloat16),
            pltpu.VMEM((whole, HD), jnp.bfloat16),
            pltpu.VMEM((whole, HD), jnp.bfloat16),
            pltpu.VMEM((whole // FRAME, HD, FRAME), jnp.bfloat16),
            pltpu.VMEM((whole // FRAME, HD, FRAME), jnp.bfloat16),
            pltpu.VMEM((SPAN * FRAME, FRAME), jnp.float32),
            pltpu.VMEM((whole, HD), jnp.float32),
            pltpu.VMEM((whole, HD), jnp.float32),
            pltpu.VMEM((heads, block, 2 * HD), jnp.float32),
            pltpu.VMEM((heads, 2, rim, 2 * HD), jnp.bfloat16),
            pltpu.VMEM((heads, 2, rim, 2 * HD), jnp.bfloat16),
            pltpu.VMEM((heads, 2, rim, 2 * HD), jnp.bfloat16),
            pltpu.SemaphoreType.DMA((heads, 2)),
            pltpu.SemaphoreType.DMA((heads, 2)),
            pltpu.SemaphoreType.DMA((heads, 2)),
            pltpu.SemaphoreType.DMA((heads, 2)),
        ],
        compiler_params=pltpu.CompilerParams(
            dimension_semantics=("arbitrary", "arbitrary"),
            collective_id=3,
            has_side_effects=True,
            vmem_limit_bytes=56 << 20,
        ),
        name="attention",
    )(bias, joined, grad_out, out_weight)


SIXTH = 512
LOW = (0, 3)
HIGH = (3, 6)


def cols(span):
    return slice(span[0] * SIXTH, span[1] * SIXTH)


def ring_places():
    me = lax.axis_index("tensor")
    z, x = me // 4, me % 4

    def place(other, shift):
        return ((z + other) % 2) * 4 + (x + shift) % 4

    return place


def meet(neighbours):
    barrier = pltpu.get_barrier_semaphore()
    for neighbour in neighbours:
        pl.semaphore_signal(
            barrier, inc=1, device_id={"tensor": neighbour}, device_id_type=pl.DeviceIdType.MESH
        )
    pl.semaphore_wait(barrier, len(neighbours))


def gather_kernel(
    gate, block, cotangent, weight, out_weight, joined, grad_out,
    out, held_cotangent, held_weight, held_out_weight, send, recv, own_sem, loads,
):
    fetches = []
    for number, (source, target) in enumerate(
        ((cotangent, held_cotangent), (out_weight, held_out_weight), (weight, held_weight))
    ):
        fetches.append(pltpu.make_async_copy(source, target, loads.at[number]))
        fetches[-1].start()
    place = ring_places()
    up, down, across = place(0, 1), place(0, -1), place(1, 0)
    size = block.shape[0]

    def rows(other, shift):
        return pl.ds(pl.multiple_of(place(other, shift) * size, size), size)

    meet((up, down, across))
    started = []

    def push(number, target, source, other, shift, span):
        where = out.at[rows(other, shift), cols(span)]
        if source is None:
            source = where
        else:
            source = source.at[:, cols(span)]
        copy = pltpu.make_async_remote_copy(
            src_ref=source,
            dst_ref=where,
            send_sem=send.at[number],
            recv_sem=recv.at[number],
            device_id={"tensor": target},
            device_id_type=pl.DeviceIdType.MESH,
        )
        copy.start()
        started.append(copy)

    def arrived(number, other, shift, span):
        where = out.at[rows(other, shift), cols(span)]
        pltpu.make_async_remote_copy(
            src_ref=where,
            dst_ref=where,
            send_sem=send.at[number],
            recv_sem=recv.at[number],
            device_id={"tensor": up},
            device_id_type=pl.DeviceIdType.MESH,
        ).wait_recv()

    push(0, up, block, 0, 0, LOW)
    push(5, down, block, 0, 0, HIGH)
    push(10, across, block, 0, 0, HIGH)
    push(1, up, block, 0, 0, HIGH)
    push(6, down, block, 0, 0, LOW)
    push(11, across, block, 0, 0, LOW)
    own = pltpu.make_async_copy(block, out.at[rows(0, 0), :], own_sem)
    own.start()
    fetches[0].wait()
    fetches[1].wait()

    def grad_rows(step, carry):
        chunk = pl.ds(pl.multiple_of(step * FRAME, FRAME), FRAME)
        scaled = (held_cotangent[chunk, :].astype(jnp.float32) * gate[...]).astype(jnp.bfloat16)
        for head in range(HELD):
            grad_out[head, chunk, :] = dot(scaled, held_out_weight[head], NT).astype(jnp.bfloat16)
        return carry

    lax.fori_loop(0, 8 * size // FRAME, grad_rows, 0)

    def join(other, shift):
        for head in range(HELD):
            product = dot(out[rows(other, shift), :], held_weight[head], NN)
            joined[head, rows(other, shift), :] = product.astype(jnp.bfloat16)

    arrived(0, 0, -1, LOW)
    push(2, up, None, 0, -1, LOW)
    push(12, across, None, 0, -1, LOW)
    arrived(5, 0, 1, HIGH)
    push(7, down, None, 0, 1, HIGH)
    arrived(10, 1, 0, HIGH)
    push(3, up, None, 1, 0, HIGH)
    push(8, down, None, 1, 0, HIGH)
    own.wait()
    fetches[2].wait()
    join(0, 0)
    arrived(6, 0, 1, LOW)
    push(13, across, None, 0, 1, LOW)
    arrived(1, 0, -1, HIGH)
    join(0, -1)
    join(0, 1)
    arrived(11, 1, 0, LOW)
    join(1, 0)
    arrived(12, 1, -1, LOW)
    push(4, up, None, 1, -1, (0, 2))
    arrived(7, 0, 2, HIGH)
    push(14, across, None, 0, 2, (4, 6))
    arrived(13, 1, 1, LOW)
    arrived(8, 1, 1, HIGH)
    push(9, down, None, 1, 1, (2, 4))
    join(1, 1)
    arrived(2, 0, 2, LOW)
    join(0, 2)
    arrived(3, 1, -1, HIGH)
    join(1, -1)
    arrived(4, 1, 2, (0, 2))
    arrived(9, 1, 2, (2, 4))
    arrived(14, 1, 2, (4, 6))
    join(1, 2)
    for copy in started:
        copy.wait_send()


def gather_rows(gate, block, cotangent, weight, out_weight):
    size, width = block.shape
    in_vmem = pl.BlockSpec(memory_space=pltpu.VMEM)
    anywhere = pl.BlockSpec(memory_space=pl.ANY)
    return pl.pallas_call(
        gather_kernel,
        out_shape=(
            jax.ShapeDtypeStruct((HELD, 8 * size, 3 * HD), block.dtype),
            jax.ShapeDtypeStruct((HELD, 8 * size, HD), block.dtype),
        ),
        in_specs=[in_vmem, in_vmem, anywhere, anywhere, anywhere],
        out_specs=(in_vmem, in_vmem),
        scratch_shapes=[
            pltpu.VMEM((8 * size, width), block.dtype),
            pltpu.VMEM(cotangent.shape, cotangent.dtype),
            pltpu.VMEM(weight.shape, weight.dtype),
            pltpu.VMEM(out_weight.shape, out_weight.dtype),
            pltpu.SemaphoreType.DMA((15,)),
            pltpu.SemaphoreType.DMA((15,)),
            pltpu.SemaphoreType.DMA(()),
            pltpu.SemaphoreType.DMA((3,)),
        ],
        compiler_params=pltpu.CompilerParams(
            collective_id=0, has_side_effects=True, vmem_limit_bytes=48 << 20
        ),
        name="gather_rows",
    )(gate.reshape(1, width), block, cotangent, weight, out_weight)


def scatter_kernel(partial, out, landing, staged, send, recv):
    place = ring_places()
    up, down, across = place(0, 1), place(0, -1), place(1, 0)
    size = out.shape[0]

    def rows(other, shift):
        return pl.ds(pl.multiple_of(place(other, shift) * size, size), size)

    meet((up, down, across))
    started = []

    def push(number, target, source, width):
        copy = pltpu.make_async_remote_copy(
            src_ref=source,
            dst_ref=landing.at[number, :, 0 : width * SIXTH],
            send_sem=send.at[number],
            recv_sem=recv.at[number],
            device_id={"tensor": target},
            device_id_type=pl.DeviceIdType.MESH,
        )
        copy.start()
        started.append(copy)

    def plain(number, target, other, shift, span):
        push(number, target, partial.at[rows(other, shift), cols(span)], span[1] - span[0])

    def arrived(number, width=3):
        where = landing.at[number, :, 0 : width * SIXTH]
        pltpu.make_async_remote_copy(
            src_ref=where,
            dst_ref=where,
            send_sem=send.at[number],
            recv_sem=recv.at[number],
            device_id={"tensor": up},
            device_id_type=pl.DeviceIdType.MESH,
        ).wait_recv()

    def summed(number, target, slot, other, shift, span, parts):
        for piece in range(span[0], span[1]):
            total = partial[rows(other, shift), cols((piece, piece + 1))].astype(jnp.float32)
            for landed, first, over in parts:
                if over[0] <= piece < over[1]:
                    total += landing[landed, :, cols((piece - first, piece - first + 1))].astype(jnp.float32)
            staged[slot, :, cols((piece - span[0], piece - span[0] + 1))] = total.astype(jnp.bfloat16)
        push(number, target, staged.at[slot], 3)

    plain(0, down, 1, 2, (0, 2))
    plain(5, up, 1, 2, (2, 4))
    plain(10, across, 1, 2, (4, 6))
    plain(1, down, 1, -1, HIGH)
    plain(2, down, 0, 2, LOW)
    plain(3, down, 0, -1, HIGH)
    arrived(5, 2)
    summed(6, up, 0, 1, 1, HIGH, ((5, 2, (2, 4)),))
    arrived(0, 2)
    summed(11, across, 1, 1, -1, LOW, ((0, 0, (0, 2)),))
    arrived(10, 2)
    summed(7, up, 2, 0, 2, HIGH, ((10, 4, (4, 6)),))
    summed(12, across, 3, 1, 1, LOW, ((5, 2, (2, 4)),))
    plain(13, across, 1, 0, LOW)
    arrived(2)
    arrived(11)
    summed(4, down, 4, 0, -1, LOW, ((2, 0, LOW), (11, 0, LOW)))
    arrived(12)
    summed(8, up, 5, 0, 1, LOW, ((12, 0, LOW),))
    arrived(7)
    summed(9, up, 6, 0, 1, HIGH, ((7, 3, HIGH),))
    arrived(1)
    arrived(6)
    summed(14, across, 7, 1, 0, HIGH, ((1, 3, HIGH), (6, 3, HIGH)))
    arrived(4)
    arrived(8)
    arrived(13)
    for piece in range(3):
        total = partial[rows(0, 0), cols((piece, piece + 1))].astype(jnp.float32)
        for landed in (4, 8, 13):
            total += landing[landed, :, cols((piece, piece + 1))].astype(jnp.float32)
        out[:, cols((piece, piece + 1))] = total
    arrived(3)
    arrived(9)
    arrived(14)
    for piece in range(3):
        total = partial[rows(0, 0), cols((piece + 3, piece + 4))].astype(jnp.float32)
        for landed in (3, 9, 14):
            total += landing[landed, :, cols((piece, piece + 1))].astype(jnp.float32)
        out[:, cols((piece + 3, piece + 4))] = total
    for copy in started:
        copy.wait_send()


def scatter_rows(partial, collective_id, name):
    height, width = partial.shape
    size = height // 8
    return pl.pallas_call(
        scatter_kernel,
        out_shape=jax.ShapeDtypeStruct((size, width), jnp.float32),
        in_specs=[pl.BlockSpec(memory_space=pltpu.VMEM)],
        out_specs=pl.BlockSpec(memory_space=pltpu.VMEM),
        scratch_shapes=[
            pltpu.VMEM((15, size, width // 2), jnp.bfloat16),
            pltpu.VMEM((8, size, width // 2), jnp.bfloat16),
            pltpu.SemaphoreType.DMA((15,)),
            pltpu.SemaphoreType.DMA((15,)),
        ],
        compiler_params=pltpu.CompilerParams(
            collective_id=collective_id, has_side_effects=True, vmem_limit_bytes=40 << 20
        ),
        cost_estimate=pl.CostEstimate(
            flops=0, bytes_accessed=180 << 20, transcendentals=0
        ),
        name=name,
    )(partial)


def on_device(
    activations, mod_gain, mod_shift, out_gate, qkv_weight, out_weight, tile_mask, cotangent
):
    shard_rows = activations.shape[0]
    frame_count = tile_mask.shape[0]
    standard, inverse, modulated = norm_rows(activations, mod_gain, mod_shift)
    weight = jnp.transpose(qkv_weight, (1, 0, 2))
    joined, grad_out = gather_rows(out_gate, modulated, cotangent, weight, out_weight)
    count = lax.axis_size("tm")
    bias = mask_bias(tile_mask, lax.axis_index("tm") * frame_count, frame_count * count)
    projected, grad_queries, grad_pairs = attention(
        joined, grad_out, bias, out_weight.reshape(-1, out_weight.shape[2])
    )
    projection = scatter_rows(projected, 1, "scatter_out")
    layer_out = (activations.astype(jnp.float32) + out_gate * projection).astype(jnp.bfloat16)
    grad_joined = jnp.concatenate([grad_queries, grad_pairs], axis=-1)
    grad_rows = jnp.einsum("hrc,hdc->rd", grad_joined, weight, preferred_element_type=jnp.float32)
    grad_norm = scatter_rows(grad_rows.astype(jnp.bfloat16), 2, "scatter_grad")
    own_cotangent = lax.dynamic_slice_in_dim(
        cotangent, lax.axis_index("tensor") * shard_rows, shard_rows, 0
    )
    input_grad = norm_back(grad_norm, standard, inverse, mod_gain, own_cotangent)
    return (layer_out, input_grad)


def solution(mesh):
    placed = (
        P(("tm", "tensor"), None),
        P(),
        P(),
        P(),
        P(None, "tensor", None),
        P("tensor", None, None),
        P("tm", None, None, None),
        P("tm", None),
    )
    return jax.shard_map(
        on_device,
        mesh=mesh,
        in_specs=placed,
        out_specs=(P(("tm", "tensor"), None), P(("tm", "tensor"), None)),
        check_vma=False,
    )
```
